32 devices in a mesh: bx: 4 (over z), by: 8 (over y, x, core).
Axes of the slice: x: 2, y: 2, z: 4, core: 2. Of those that a mesh axis runs over, the one named last changes fastest.
Arguments:
- field_now: float32 [4, 64, 256, 256], P(None, 'bx', 'by'), may hold values from -6 to 6
- field_before: float32 [4, 64, 256, 256], P(None, 'bx', 'by'), may hold values from -6 to 6
- interp_weight: bfloat16 [4096, 512, 128], P(('bx', 'by')), may hold values from -0.25 to 0.25
- tile_index: int32 [4096], P(('bx', 'by')), may hold values from 0 to 255
- step_offset: int32 [4096], P(('bx', 'by')), may hold values from 0 to 3
- block_patch: int32 [4096], P(('bx', 'by')), may hold values from 0 to 2047, as said below
- ownership: int32 [2048], replicated, may hold values from 0 to 2047, as said below
- near_pairs: int32 [4096, 2], P(('bx', 'by')), may hold values from 0 to 63
- precorrection: bfloat16 [4096, 128, 128], P(('bx', 'by')), may hold values from -0.375 to 0.375
Outputs:
- patch_field: float32 [2048, 4, 128], P(('bx', 'by'))
The draws below stay inside these ranges and needn't reach their ends.
Inputs may be any that keep to these rules, and one draw needn't show every extreme that they name: `ownership`: a permutation; patch p is owned by device ownership[p] // 64 (device index bx * 8 + by) as its local patch ownership[p] % 64. `block_patch`: the blocks of one device feed at most 8 patches counted with repetition of any one owner; some owner receives exactly 8 blocks from every device.
All inputs are finite; a program needn't handle non-finite values.
Results may differ from the reference program's by a relative error of at most 0.0035.
Values sent between devices are 32-bit elements; how exact they have to be, the bound alone decides.
No kernel may reach another device: no remote copies, remote signals or barrier semaphores. Data moves between devices by JAX's collectives and lax.ppermute only.
A program may use at most 128 MiB of HBM per device.

```python
import jax
import jax.numpy as jnp
from jax import lax

COMP = 4
PATCH_PTS = 128
CX = 16
CY = 32
NZ = 256
STEPS = 4
BLK_DEV = 128
PATCH_DEV = 64
NEAR_DEV = 128
CAP = 8
PATCHES = 2048
NX = 64
NY = 256
TILES_DEV = 256
N_BX = 4
N_BY = 8
DEVICES = 32


def owner_table(key):
    return jax.random.permutation(jax.random.fold_in(key, 11), PATCHES).astype(jnp.int32)


def draw_ownership(key, part):
    return owner_table(key)


def draw_block_patch(key, part):
    slots = DEVICES * CAP
    table = owner_table(key)
    inverse = jnp.zeros((PATCHES,), jnp.int32).at[table].set(jnp.arange(PATCHES, dtype=jnp.int32))
    forced = jax.random.randint(jax.random.fold_in(key, 12), (), 0, DEVICES)

    def one_device(device):
        seeds = jax.random.split(jax.random.fold_in(jax.random.fold_in(key, 13), device), 3)
        places = jnp.arange(slots, dtype=jnp.int32)
        score = jax.random.randint(seeds[0], (slots,), 0, 2 ** 20) * slots + places
        score = jnp.where(places // CAP == forced, places - slots, score)
        chosen = jnp.argsort(score)[:BLK_DEV].astype(jnp.int32)
        chosen = jax.random.permutation(seeds[1], chosen)
        local = jax.random.randint(seeds[2], (BLK_DEV,), 0, PATCH_DEV)
        return inverse[chosen // CAP * PATCH_DEV + local]
    return jax.vmap(one_device)(jnp.arange(DEVICES, dtype=jnp.int32)).reshape(-1).astype(jnp.int32)


def set_ends(drawn, stream_key, smallest, largest):
    longest = drawn.shape.index(max(drawn.shape))
    spots = []
    for shift in (0, 1):
        where = [jax.random.randint(jax.random.fold_in(stream_key, axis), (), 0, length) for axis, length in enumerate(drawn.shape)]
        where[longest] = (where[longest] + shift) % drawn.shape[longest]
        spots.append(tuple(where))
    return drawn.at[spots[0]].set(smallest).at[spots[1]].set(largest)


def level_of(rng, shape, cuts, least, largest):
    def one(axis_at, blocks):
        heights = jax.random.uniform(jax.random.fold_in(jax.random.fold_in(rng, 6), axis_at), (blocks,), jnp.float32, least / len(cuts), largest / len(cuts))
        return jnp.repeat(jnp.exp(heights), shape[axis_at] // blocks).reshape((-1,) + (1,) * (len(shape) - axis_at - 1))

    gain = one(*cuts[0])
    for cut in cuts[1:]:
        gain = gain * one(*cut)
    return gain


def normal_values(key, dims, width, most, shards=(), held_as=jnp.bfloat16):
    gain = level_of(key, dims, shards, -0.22, 0.18) if shards else 1.0
    drawn = jax.random.normal(key, dims, jnp.float32) * width * gain
    return jnp.minimum(jnp.maximum(drawn, -most), most).astype(held_as)


def setup_inputs(seed: int = 0) -> dict:
    splits = jax.random.split(jax.random.key(seed), 10)
    field_now = normal_values(splits[0], (COMP, NX, NY, NZ), 1.0, 6.0, ((1, 4), (2, 8)), jnp.float32)
    field_before = normal_values(splits[1], (COMP, NX, NY, NZ), 1.0, 6.0, ((1, 4), (2, 8)), jnp.float32)
    interp_weight = normal_values(splits[2], (DEVICES * BLK_DEV, 512, PATCH_PTS), 512 ** -0.5, 0.25, ((0, 32),))
    tile_index = set_ends(jax.random.randint(splits[3], (DEVICES * BLK_DEV,), 0, TILES_DEV), jax.random.fold_in(splits[3], 1), 0, TILES_DEV - 1).astype(jnp.int32)
    step_offset = set_ends(jax.random.randint(splits[4], (DEVICES * BLK_DEV,), 0, STEPS), jax.random.fold_in(splits[4], 1), 0, STEPS - 1).astype(jnp.int32)
    block_patch = draw_block_patch(jax.random.fold_in(splits[9], 71), 0)
    ownership = draw_ownership(jax.random.fold_in(splits[9], 71), 0)
    near_pairs = set_ends(jax.random.randint(splits[7], (DEVICES * NEAR_DEV, 2), 0, PATCH_DEV), jax.random.fold_in(splits[7], 1), 0, PATCH_DEV - 1).astype(jnp.int32)
    precorrection = normal_values(splits[8], (DEVICES * NEAR_DEV, PATCH_PTS, PATCH_PTS), (2 * PATCH_PTS) ** -0.5, 0.375, ((0, 32),))
    return dict(field_now=field_now, field_before=field_before, interp_weight=interp_weight, tile_index=tile_index, step_offset=step_offset, block_patch=block_patch, ownership=ownership, near_pairs=near_pairs, precorrection=precorrection)


COEF = 0.3


def advance(now, before):
    padded = jnp.pad(now, ((0, 0), (1, 1), (1, 1), (1, 1)))
    beside = padded[:, 2:, 1:-1, 1:-1] + padded[:, :-2, 1:-1, 1:-1]
    beside = beside + padded[:, 1:-1, 2:, 1:-1] + padded[:, 1:-1, :-2, 1:-1]
    beside = beside + padded[:, 1:-1, 1:-1, 2:] + padded[:, 1:-1, 1:-1, :-2]
    return 2.0 * now - before + COEF * (beside - 6.0 * now)


def reference(field_now, field_before, interp_weight, tile_index, step_offset, block_patch, ownership, near_pairs, precorrection):
    devices = N_BX * N_BY
    tiles_y = CY // 8
    tiles_z = NZ // 8
    tiles_x = CX // 8
    device_of = jnp.arange(devices * BLK_DEV, dtype=jnp.int32) // BLK_DEV
    brick_x = device_of // N_BY
    brick_y = device_of % N_BY
    local_x = tile_index // (tiles_y * tiles_z)
    local_y = (tile_index // tiles_z) % tiles_y
    local_z = tile_index % tiles_z
    global_tile = ((brick_x * tiles_x + local_x) * (tiles_y * N_BY) + brick_y * tiles_y + local_y) * tiles_z + local_z
    global_tile = global_tile.astype(jnp.int32)
    picked = jnp.zeros((devices * BLK_DEV, COMP, 512), jnp.bfloat16)
    now, before = field_now, field_before
    for step in range(STEPS):
        fresh = advance(now, before)
        tiles = fresh.reshape(COMP, NX // 8, 8, NY // 8, 8, NZ // 8, 8)
        tiles = tiles.transpose(1, 3, 5, 0, 2, 4, 6).reshape(-1, COMP, 512).astype(jnp.bfloat16)
        picked = jnp.where((step_offset == step)[:, None, None], tiles[global_tile], picked)
        before, now = now, fresh

    def interpolate(pair):
        tile_rows, weights = pair
        return jnp.einsum("bcn,bnm->bcm", tile_rows.astype(jnp.float32), weights.astype(jnp.float32))

    panels = lax.map(interpolate, (picked.reshape(devices, BLK_DEV, COMP, 512), interp_weight.reshape(devices, BLK_DEV, 512, PATCH_PTS)))
    target = ownership[block_patch].astype(jnp.int32)
    field = jax.ops.segment_sum(panels.reshape(devices * BLK_DEV, COMP * PATCH_PTS), target, num_segments=PATCHES)
    field = field.reshape(devices, PATCH_DEV, COMP, PATCH_PTS)

    def correct(triple):
        owned, pairs, blocks = triple
        source = owned.astype(jnp.bfloat16)[pairs[:, 1]].astype(jnp.float32)
        terms = jnp.einsum("kcn,knm->kcm", source, blocks.astype(jnp.float32))
        return owned + jax.ops.segment_sum(terms, pairs[:, 0], num_segments=PATCH_DEV)

    result = lax.map(correct, (field, near_pairs.reshape(devices, NEAR_DEV, 2), precorrection.reshape(devices, NEAR_DEV, PATCH_PTS, PATCH_PTS)))
    return result.reshape(PATCHES, COMP, PATCH_PTS)
```

```python
import functools

import jax
import jax.numpy as jnp
from jax import lax
from jax.experimental import pallas as pl
from jax.experimental.pallas import tpu as pltpu
from jax.sharding import PartitionSpec as P

STEPS = 4
COEF = 0.3
LANES = 128
TILE = 8
OWN = 8
MEGA = 1 << 20


def ceil8(n):
    return (n + 7) // 8 * 8


def edge_rows():
    at_low = lax.axis_index("by") == 0
    at_high = lax.axis_index("by") == lax.axis_size("by") - 1
    row = lax.broadcasted_iota(jnp.int32, (8, LANES), 0)
    keep_low = row >= jnp.where(at_low, STEPS, 0)
    keep_high = row < jnp.where(at_high, 8 - STEPS, 8)
    return keep_low, keep_high


def beside_z(mid):
    halves = len(mid)
    lane = lax.broadcasted_iota(jnp.int32, mid[0].shape, 1)
    first = lane == 0
    last = lane == LANES - 1
    up = [pltpu.roll(m, 1, 1) for m in mid]
    down = [pltpu.roll(m, LANES - 1, 1) for m in mid]
    sums = []
    for h in range(halves):
        below = jnp.where(first, up[h - 1] if h else 0.0, up[h])
        above = jnp.where(last, down[h + 1] if h + 1 < halves else 0.0, down[h])
        sums.append(below + above)
    return sums


def rows_of(ref, h, c, slot, rows):
    return ref[h, c, slot, OWN - STEPS : OWN - STEPS + rows, :]


def advance(cur, old, c, slot, beside, edges, rows, keep=None):
    halves = cur.shape[0]
    start = OWN - STEPS
    mid = [cur[h, c, slot, start : start + rows, :] for h in range(halves)]
    across = beside_z(mid)
    for h in range(halves):
        total = across[h] + cur[h, c, slot, start - 1 : start - 1 + rows, :]
        total = total + cur[h, c, slot, start + 1 : start + 1 + rows, :]
        for ref, place in beside:
            total = total + rows_of(ref, h, c, place, rows)
        fresh = (2.0 - 6.0 * COEF) * mid[h] - rows_of(old, h, c, slot, rows) + COEF * total
        if keep is not None:
            fresh = jnp.where(keep, fresh, 0.0)
        old[h, c, slot, start : start + 8, :] = jnp.where(edges[0], fresh[:8], 0.0)
        old[h, c, slot, start + 8 : start + rows - 8, :] = fresh[8 : rows - 8]
        old[h, c, slot, start + rows - 8 : start + rows, :] = jnp.where(
            edges[1], fresh[rows - 8 :], 0.0
        )


def fill_rows(now, before, c, slot, y_low, y_high, x, size_y):
    for h in range(now.shape[0]):
        z = slice(h * LANES, (h + 1) * LANES)
        top = OWN + size_y
        now[h, c, slot, OWN - STEPS : OWN, :] = y_low[c, x, :STEPS, z]
        before[h, c, slot, OWN - STEPS : OWN, :] = y_low[c, x, STEPS:, z]
        now[h, c, slot, top : top + STEPS, :] = y_high[c, x, :STEPS, z]
        before[h, c, slot, top : top + STEPS, :] = y_high[c, x, STEPS:, z]


def faces_kernel(now, before, y_low, y_high, out_low, out_high, p_now, p_before, sems, *, size_y):
    comps, size_x, _, size_z = now.shape
    halves = size_z // LANES
    rows = size_y + 2 * STEPS
    near = STEPS
    copies = []
    for a, (src, dst) in enumerate(((now, p_now), (before, p_before))):
        for face in range(2):
            x0 = 0 if face == 0 else size_x - near
            s0 = 2 if face == 0 else 6
            for h in range(halves):
                copies.append(
                    pltpu.make_async_copy(
                        src.at[:, x0 : x0 + near, :, h * LANES : (h + 1) * LANES],
                        dst.at[h, :, s0 : s0 + near, OWN : OWN + size_y, :],
                        sems.at[a, face, h],
                    )
                )
    for copy in copies:
        copy.start()

    def slot(face, depth):
        return depth + 2 if face == 0 else 9 - depth

    edges = edge_rows()
    outs = (out_low, out_high)

    def prepare(c, carry):
        for face in range(2):
            for depth in range(near):
                x = depth if face == 0 else size_x - 1 - depth
                fill_rows(p_now, p_before, c, slot(face, depth), y_low, y_high, x, size_y)
            for depth in (-1, -2):
                for h in range(halves):
                    zero = jnp.zeros((rows + 8, LANES), jnp.float32)
                    p_now[h, c, slot(face, depth)] = zero
                    p_before[h, c, slot(face, depth)] = zero
        return carry

    lax.fori_loop(0, comps, prepare, 0)
    for copy in copies:
        copy.wait()

    def give(buf, c, step, offset):
        more = STEPS - 1 - step
        for face in range(2):
            place = slot(face, 0)
            for h in range(halves):
                outs[face][c, h, step * size_y : (step + 1) * size_y, :] = buf[
                    h, c, place, OWN : OWN + size_y, :
                ]
                if more:
                    base = STEPS * size_y + offset
                    outs[face][c, h, base : base + more, :] = buf[h, c, place, OWN - more : OWN, :]
                    outs[face][c, h, base + more : base + 2 * more, :] = buf[
                        h, c, place, OWN + size_y : OWN + size_y + more, :
                    ]

    def evolve(c, carry):
        cur, old = p_now, p_before
        give(cur, c, 0, 0)
        offset = 2 * (STEPS - 1)
        for step, depths in ((1, (-1, 0, 1, 2)), (2, (-1, 0, 1)), (3, (0,))):
            for face in range(2):
                for depth in depths:
                    place = slot(face, depth)
                    advance(
                        cur, old, c, place, ((cur, place - 1), (cur, place + 1)), edges, rows
                    )
            cur, old = old, cur
            give(cur, c, step, offset)
            offset += 2 * (STEPS - 1 - step)
        for face in range(2):
            for h in range(halves):
                base = STEPS * size_y + offset
                outs[face][c, h, base : base + 4, :] = jnp.zeros((4, LANES), jnp.float32)
        return carry

    lax.fori_loop(0, comps, evolve, 0)


def identity(n, dtype):
    row = lax.broadcasted_iota(jnp.int32, (n, n), 0)
    col = lax.broadcasted_iota(jnp.int32, (n, n), 1)
    return (row == col).astype(jnp.float32).astype(dtype)


def turn_tile(buf, x0, count_x, y0, eye):
    halves, comps = buf.shape[:2]
    parts = []
    for h in range(halves):
        cells = buf[h, :, pl.ds(x0, count_x), pl.ds(y0, TILE), :]
        parts.append(cells.reshape(comps * count_x * TILE, LANES).astype(jnp.bfloat16))
    cells = jnp.concatenate(parts, axis=1)
    return lax.dot_general(
        eye, cells, (((1,), (1,)), ((), ())), preferred_element_type=jnp.float32
    )


def fill_spread(spread, comps, planes):
    rows, cols = spread.shape
    per = planes * TILE * TILE
    for c in range(comps):
        row = lax.broadcasted_iota(jnp.int32, (rows, per), 0)
        col = lax.broadcasted_iota(jnp.int32, (rows, per), 1)
        hot = row == col // TILE + c * planes * TILE
        spread[:, c * per : (c + 1) * per] = hot.astype(jnp.float32).astype(jnp.bfloat16)


def spread_group(table, index, spread, comps, group):
    cells = jnp.concatenate([table[index(b)] for b in range(group)], axis=0)
    wide = jnp.dot(
        cells.astype(jnp.bfloat16), spread[...], preferred_element_type=jnp.float32
    )
    row = lax.broadcasted_iota(jnp.int32, wide.shape, 0) % TILE
    col = lax.broadcasted_iota(jnp.int32, wide.shape, 1) % TILE
    wide = jnp.where(row == col, wide, 0.0)
    per = wide.shape[1] // comps
    return [
        jnp.concatenate(
            [wide[b * TILE : (b + 1) * TILE, c * per : (c + 1) * per] for c in range(comps)],
            axis=0,
        ).astype(jnp.bfloat16)
        for b in range(group)
    ]


GROUP = 8


def own_kernel(
    tile_index, step_offset, now, before, y_low, y_high, weight, out,
    p_now, p_before, table, held, spread, sems, wsems,
):
    comps, size_x, size_y, size_z = now.shape
    halves = size_z // LANES
    rows = size_y + 2 * STEPS
    blocks = weight.shape[0]
    tiles_y = size_y // TILE
    tiles_z = size_z // TILE
    columns = size_x // TILE * tiles_y
    copies = []
    for a, (src, dst) in enumerate(((now, p_now), (before, p_before))):
        for h in range(halves):
            copies.append(
                pltpu.make_async_copy(
                    src.at[:, :, :, h * LANES : (h + 1) * LANES],
                    dst.at[h, :, 2 : 2 + size_x, OWN : OWN + size_y, :],
                    sems.at[a, h],
                )
            )
    for copy in copies:
        copy.start()

    def weights(g):
        part = pl.ds(g * GROUP, GROUP)
        return pltpu.make_async_copy(weight.at[part], held.at[part], wsems.at[g])

    def start(g, carry):
        weights(g).start()
        return carry

    lax.fori_loop(0, blocks // GROUP, start, 0)
    edges = edge_rows()
    keep_low = lax.axis_index("bx") > 0
    keep_high = lax.axis_index("bx") < lax.axis_size("bx") - 1

    def prepare(c, carry):
        def one(x, carry):
            fill_rows(p_now, p_before, c, x + 2, y_low, y_high, x, size_y)
            return carry

        lax.fori_loop(0, size_x, one, 0)
        for place in (0, 1, size_x + 2, size_x + 3):
            for h in range(halves):
                zero = jnp.zeros((rows + 8, LANES), jnp.float32)
                p_now[h, c, place] = zero
                p_before[h, c, place] = zero
        return carry

    lax.fori_loop(0, comps, prepare, 0)
    fill_spread(spread, comps, TILE)
    eye = identity(size_z, jnp.bfloat16)
    for copy in copies:
        copy.wait()
    cur, old = p_now, p_before
    for step in range(STEPS):
        out_planes = (1, 2, 1, 0)[step]

        def evolve(c, carry, cur=cur, old=old, out_planes=out_planes):
            def inner(x, carry):
                place = x + 2
                advance(cur, old, c, place, ((cur, place - 1), (cur, place + 1)), edges, rows)
                return carry

            lax.fori_loop(0, size_x, inner, 0)
            for depth in range(1, out_planes + 1):
                for face in range(2):
                    place = 2 - depth if face == 0 else size_x + 1 + depth
                    inward = place + 1 if face == 0 else place - 1
                    outward = place - 1 if face == 0 else place + 1
                    beside = [(cur, inward)]
                    if depth < 2:
                        beside.append((cur, outward))
                    advance(
                        cur, old, c, place, beside, edges, rows, keep_high if face else keep_low
                    )
            return carry

        lax.fori_loop(0, comps, evolve, 0)

        def turn(column, carry, fresh=old, step=step):
            x0 = 2 + column // tiles_y * TILE
            y0 = OWN + column % tiles_y * TILE
            turned = turn_tile(fresh, x0, TILE, pl.multiple_of(y0, TILE), eye)
            first = (step * columns + column) * tiles_z
            table[pl.ds(first, tiles_z)] = turned.reshape(tiles_z, TILE, comps * TILE * TILE)
            return carry

        lax.fori_loop(0, columns, turn, 0)
        cur, old = old, cur

    def panels(g, carry):
        weights(g).wait()

        def index(b):
            block = g * GROUP + b
            return step_offset[block] * (columns * tiles_z) + tile_index[block]

        lhs = spread_group(table, index, spread, comps, GROUP)
        for b in range(GROUP):
            made = jnp.dot(lhs[b], held[g * GROUP + b], preferred_element_type=jnp.float32)
            for c in range(comps):
                total = jnp.sum(made[c * TILE : (c + 1) * TILE], axis=0, keepdims=True)
                out[pl.ds(g * GROUP * comps + b * comps + c, 1), :] = total
        return carry

    lax.fori_loop(0, blocks // GROUP, panels, 0)


def share_kernel(
    tile_index, step_offset, block_patch, ownership, from_low, from_high, weight, own_panels, out,
    bound, d_now, d_before, table, held, spread, count, wsems,
    *, size_x, size_y, size_z, slots, stride,
):
    comps = from_low.shape[0]
    halves = size_z // LANES
    rows = size_y + 2 * STEPS
    blocks = weight.shape[0]
    tiles_y = size_y // TILE
    tiles_z = size_z // TILE
    columns = 2 * tiles_y
    devices = lax.axis_size("bx") * lax.axis_size("by")
    owned = ownership.shape[0] // devices
    part = STEPS * TILE * TILE

    def weights(b):
        face = tile_index[b] // (tiles_y * tiles_z)
        return pltpu.make_async_copy(
            weight.at[b, pl.ds(pl.multiple_of(face * part, part), part), :],
            held.at[b],
            wsems.at[b],
        )

    def start(b, carry):
        weights(b).start()
        return carry

    lax.fori_loop(0, blocks, start, 0)
    out[...] = jnp.full(out.shape, -1.0, jnp.float32)

    def clear(d, carry):
        count[d] = 0
        return carry

    lax.fori_loop(0, devices, clear, 0)
    edges = edge_rows()
    froms = (from_low, from_high)

    def prepare(c, carry):
        for face in range(2):
            offset = STEPS * size_y
            for step in range(STEPS):
                place = face * STEPS + step
                more = STEPS - 1 - step
                for h in range(halves):
                    src = froms[face]
                    bound[h, c, place, OWN : OWN + size_y, :] = src[
                        c, h, step * size_y : (step + 1) * size_y, :
                    ]
                    if more:
                        bound[h, c, place, OWN - more : OWN, :] = src[
                            c, h, offset : offset + more, :
                        ]
                        bound[h, c, place, OWN + size_y : OWN + size_y + more, :] = src[
                            c, h, offset + more : offset + 2 * more, :
                        ]
                offset += 2 * more
            for place in range(face * STEPS, (face + 1) * STEPS):
                for h in range(halves):
                    zero = jnp.zeros((rows + 8, LANES), jnp.float32)
                    d_now[h, c, place] = zero
                    d_before[h, c, place] = zero
        return carry

    lax.fori_loop(0, comps, prepare, 0)
    fill_spread(spread, comps, STEPS)
    eye = identity(size_z, jnp.bfloat16)

    def slot(face, depth):
        return depth if face == 0 else 2 * STEPS - 1 - depth

    cur, old = d_now, d_before
    for step in range(STEPS):

        def evolve(c, carry, cur=cur, old=old, step=step):
            for face in range(2):
                for depth in range(step + 1):
                    if depth == 0:
                        beside = [(bound, face * STEPS + step)]
                    else:
                        beside = [(cur, slot(face, depth - 1))]
                    if depth + 1 < STEPS:
                        beside.append((cur, slot(face, depth + 1)))
                    advance(cur, old, c, slot(face, depth), beside, edges, rows)
            return carry

        lax.fori_loop(0, comps, evolve, 0)

        def turn(column, carry, fresh=old, step=step):
            x0 = column // tiles_y * STEPS
            y0 = OWN + column % tiles_y * TILE
            turned = turn_tile(fresh, x0, STEPS, pl.multiple_of(y0, TILE), eye)
            first = (step * columns + column) * tiles_z
            table[pl.ds(first, tiles_z)] = turned.reshape(tiles_z, TILE, comps * STEPS * TILE)
            return carry

        lax.fori_loop(0, columns, turn, 0)
        cur, old = old, cur

    def panels(g, carry):
        def index(b):
            block = g * GROUP + b
            return step_offset[block] * (columns * tiles_z) + tile_index[block]

        lhs = spread_group(table, index, spread, comps, GROUP)
        for b in range(GROUP):
            block = g * GROUP + b
            weights(block).wait()
            made = jnp.dot(lhs[b], held[block], preferred_element_type=jnp.float32)
            target = ownership[block_patch[block]]
            owner = target // owned
            local = target - owner * owned
            rank = count[owner]
            count[owner] = rank + 1
            row = owner * stride + rank
            for c in range(comps):
                total = jnp.sum(made[c * TILE : (c + 1) * TILE], axis=0, keepdims=True)
                total = total + own_panels[pl.ds(block * comps + c, 1), :]
                out[pl.ds(row + c * slots, 1), :] = total
            out[pl.ds(row + comps * slots, 1), :] = jnp.full(
                (1, LANES), local.astype(jnp.float32), jnp.float32
            )
        return carry

    lax.fori_loop(0, blocks // GROUP, panels, 0)


PAIRS = 8


def near_kernel(pairs, got, precorrection, out, field, held, sems, *, comps, slots, stride):
    count = precorrection.shape[0]
    senders = got.shape[0] // stride
    owned = out.shape[0] // comps

    def blocks(g):
        part = pl.ds(g * PAIRS, PAIRS)
        return pltpu.make_async_copy(precorrection.at[part], held.at[part], sems.at[g])

    for g in range(count // PAIRS):
        blocks(g).start()
    whole = got[...].reshape(senders, stride, LANES)
    ids = whole[:, comps * slots : (comps + 1) * slots, :].reshape(senders * slots, LANES)
    ids = ids.T[:owned]
    hot = ids == lax.broadcasted_iota(jnp.int32, ids.shape, 0).astype(jnp.float32)
    hot = hot.astype(jnp.float32).astype(jnp.bfloat16)
    for c in range(comps):
        rest = whole[:, c * slots : (c + 1) * slots, :].reshape(senders * slots, LANES)
        total = None
        for _ in range(3):
            piece = rest.astype(jnp.bfloat16)
            rest = rest - piece.astype(jnp.float32)
            part = jnp.dot(hot, piece, preferred_element_type=jnp.float32)
            total = part if total is None else total + part
        field[pl.ds(c, owned, stride=comps), :] = total
        out[pl.ds(c, owned, stride=comps), :] = total

    def group(g, carry):
        blocks(g).wait()
        for b in range(PAIRS):
            k = g * PAIRS + b
            i = pairs[2 * k]
            j = pairs[2 * k + 1]
            source = field[pl.ds(j * comps, comps), :].astype(jnp.bfloat16)
            term = jnp.dot(source, held[k], preferred_element_type=jnp.float32)
            out[pl.ds(i * comps, comps), :] += term
        return carry

    lax.fori_loop(0, count // PAIRS, group, 0)


SMEM = pl.BlockSpec(memory_space=pltpu.SMEM)
VMEM = pl.BlockSpec(memory_space=pltpu.VMEM)
ANY = pl.BlockSpec(memory_space=pl.ANY)


def kernel_params(mib):
    return pltpu.CompilerParams(vmem_limit_bytes=mib * MEGA)


def per_device(
    field_now,
    field_before,
    interp_weight,
    tile_index,
    step_offset,
    block_patch,
    ownership,
    near_pairs,
    precorrection,
):
    comps, size_x, size_y, size_z = field_now.shape
    count_x = lax.axis_size("bx")
    count_y = lax.axis_size("by")
    devices = count_x * count_y
    blocks, cells, points = interp_weight.shape
    capacity = max(2, (2 * blocks + devices - 1) // devices)
    owned = ownership.shape[0] // devices
    halves = size_z // LANES
    rows = size_y + 2 * OWN
    f32, bf16 = jnp.float32, jnp.bfloat16

    def swap(up, down, axis, count):
        forward = [(i, i + 1) for i in range(count - 1)]
        backward = [(b, a) for a, b in forward]
        return lax.ppermute(up, axis, forward), lax.ppermute(down, axis, backward)

    up = jnp.concatenate([field_now[:, :, -STEPS:], field_before[:, :, -STEPS:]], axis=2)
    down = jnp.concatenate([field_now[:, :, :STEPS], field_before[:, :, :STEPS]], axis=2)
    y_low, y_high = swap(up, down, "by", count_y)

    face_rows = STEPS * size_y + ceil8(STEPS * (STEPS - 1) + 4)
    face = jax.ShapeDtypeStruct((comps, halves, face_rows, LANES), f32)
    plane = pltpu.VMEM((halves, comps, 12, rows, LANES), f32)
    give_low, give_high = pl.pallas_call(
        functools.partial(faces_kernel, size_y=size_y),
        out_shape=(face, face),
        in_specs=[ANY, ANY, VMEM, VMEM],
        out_specs=(VMEM, VMEM),
        scratch_shapes=[plane, plane, pltpu.SemaphoreType.DMA((2, 2, halves))],
        compiler_params=kernel_params(32),
    )(field_now, field_before, y_low, y_high)
    from_low, from_high = swap(give_high, give_low, "bx", count_x)

    tiles = size_x // TILE * (size_y // TILE) * (size_z // TILE)
    brick = pltpu.VMEM((halves, comps, size_x + 4, rows, LANES), f32)
    own_panels = pl.pallas_call(
        own_kernel,
        out_shape=jax.ShapeDtypeStruct((blocks * comps, points), f32),
        in_specs=[SMEM, SMEM, ANY, ANY, VMEM, VMEM, ANY],
        out_specs=VMEM,
        scratch_shapes=[
            brick,
            brick,
            pltpu.VMEM((STEPS * tiles, TILE, comps * TILE * TILE), f32),
            pltpu.VMEM((blocks, cells, points), bf16),
            pltpu.VMEM((comps * TILE * TILE, comps * cells), bf16),
            pltpu.SemaphoreType.DMA((2, halves)),
            pltpu.SemaphoreType.DMA((blocks // GROUP,)),
        ],
        compiler_params=kernel_params(52),
    )(tile_index, step_offset, field_now, field_before, y_low, y_high, interp_weight)

    slots = ceil8(capacity)
    stride = (comps + 1) * slots
    thin = pltpu.VMEM((halves, comps, 2 * STEPS, rows, LANES), f32)
    sent = pl.pallas_call(
        functools.partial(
            share_kernel,
            size_x=size_x,
            size_y=size_y,
            size_z=size_z,
            slots=slots,
            stride=stride,
        ),
        out_shape=jax.ShapeDtypeStruct((devices * stride, points), f32),
        in_specs=[SMEM, SMEM, SMEM, SMEM, VMEM, VMEM, ANY, VMEM],
        out_specs=VMEM,
        scratch_shapes=[
            thin,
            thin,
            thin,
            pltpu.VMEM((STEPS * tiles, TILE, comps * STEPS * TILE), f32),
            pltpu.VMEM((blocks, STEPS * TILE * TILE, points), bf16),
            pltpu.VMEM((comps * STEPS * TILE, comps * STEPS * TILE * TILE), bf16),
            pltpu.SMEM((devices,), jnp.int32),
            pltpu.SemaphoreType.DMA((blocks,)),
        ],
        compiler_params=kernel_params(52),
    )(
        tile_index,
        step_offset,
        block_patch,
        ownership,
        from_low,
        from_high,
        interp_weight,
        own_panels,
    )
    got = lax.all_to_all(
        sent.reshape(devices, stride, points), ("bx", "by"), 0, 0, tiled=True
    ).reshape(devices * stride, points)

    pairs = near_pairs.shape[0]
    result = pl.pallas_call(
        functools.partial(near_kernel, comps=comps, slots=slots, stride=stride),
        out_shape=jax.ShapeDtypeStruct((owned * comps, points), f32),
        in_specs=[SMEM, VMEM, ANY],
        out_specs=VMEM,
        scratch_shapes=[
            pltpu.VMEM((owned * comps, points), f32),
            pltpu.VMEM((pairs, points, points), bf16),
            pltpu.SemaphoreType.DMA((pairs // PAIRS,)),
        ],
        compiler_params=kernel_params(32),
    )(near_pairs.reshape(-1), got, precorrection)
    return result.reshape(owned, comps, points)


def solution(mesh):
    placed = (
        P(None, "bx", "by", None),
        P(None, "bx", "by", None),
        P(("bx", "by"), None, None),
        P(("bx", "by")),
        P(("bx", "by")),
        P(("bx", "by")),
        P(),
        P(("bx", "by"), None),
        P(("bx", "by"), None, None),
    )
    return jax.shard_map(
        per_device,
        mesh=mesh,
        in_specs=placed,
        out_specs=P(("bx", "by"), None, None),
        check_vma=False,
    )
```

```python
import functools

import jax
import jax.numpy as jnp
from jax import lax
from jax.experimental import pallas as pl
from jax.experimental.pallas import tpu as pltpu
from jax.sharding import PartitionSpec as P

STEPS = 4
COEF = 0.3
LANES = 128
TILE = 8
OWN = 8
MEGA = 1 << 20


def ceil8(n):
    return (n + 7) // 8 * 8


def edge_rows():
    at_low = lax.axis_index("by") == 0
    at_high = lax.axis_index("by") == lax.axis_size("by") - 1
    row = lax.broadcasted_iota(jnp.int32, (8, LANES), 0)
    keep_low = row >= jnp.where(at_low, STEPS, 0)
    keep_high = row < jnp.where(at_high, 8 - STEPS, 8)
    return keep_low, keep_high


def beside_z(mid):
    halves = len(mid)
    lane = lax.broadcasted_iota(jnp.int32, mid[0].shape, 1)
    first = lane == 0
    last = lane == LANES - 1
    up = [pltpu.roll(m, 1, 1) for m in mid]
    down = [pltpu.roll(m, LANES - 1, 1) for m in mid]
    sums = []
    for h in range(halves):
        below = jnp.where(first, up[h - 1] if h else 0.0, up[h])
        above = jnp.where(last, down[h + 1] if h + 1 < halves else 0.0, down[h])
        sums.append(below + above)
    return sums


def load(ref, c, slot, start, rows):
    return [ref[h, c, slot, start : start + rows, :] for h in range(ref.shape[0])]


def advance(cur, old, c, slot, mid, beside, edges, keep=None):
    rows = mid[0].shape[0]
    start = OWN if edges is None else OWN - STEPS
    across = beside_z(mid)
    for h in range(len(mid)):
        total = across[h] + cur[h, c, slot, start - 1 : start - 1 + rows, :]
        total = total + cur[h, c, slot, start + 1 : start + 1 + rows, :]
        for plane in beside:
            total = total + plane[h]
        before = old[h, c, slot, start : start + rows, :]
        fresh = (2.0 - 6.0 * COEF) * mid[h] - before + COEF * total
        if keep is not None:
            fresh = jnp.where(keep, fresh, 0.0)
        if edges is None:
            old[h, c, slot, start : start + rows, :] = fresh
            continue
        old[h, c, slot, start : start + 8, :] = jnp.where(edges[0], fresh[:8], 0.0)
        old[h, c, slot, start + 8 : start + rows - 8, :] = fresh[8 : rows - 8]
        old[h, c, slot, start + rows - 8 : start + rows, :] = jnp.where(
            edges[1], fresh[rows - 8 :], 0.0
        )


def fill_rows(now, before, c, slot, y_low, y_high, x, size_y):
    for h in range(now.shape[0]):
        z = slice(h * LANES, (h + 1) * LANES)
        top = OWN + size_y
        now[h, c, slot, OWN - STEPS : OWN, :] = y_low[c, x, :STEPS, z]
        before[h, c, slot, OWN - STEPS : OWN, :] = y_low[c, x, STEPS:, z]
        now[h, c, slot, top : top + STEPS, :] = y_high[c, x, :STEPS, z]
        before[h, c, slot, top : top + STEPS, :] = y_high[c, x, STEPS:, z]


def faces_kernel(near_now, near_before, y_low, y_high, out_low, out_high, p_now, p_before):
    halves, comps, _, size_y, _ = near_now.shape
    size_x = y_low.shape[1]
    rows = size_y + 2 * STEPS
    near = STEPS

    def slot(face, depth):
        return depth + 2 if face == 0 else 9 - depth

    edges = edge_rows()
    outs = (out_low, out_high)

    def prepare(c, carry):
        for face in range(2):
            for depth in range(near):
                x = depth if face == 0 else size_x - 1 - depth
                place = depth if face == 0 else 2 * near - 1 - depth
                for h in range(halves):
                    own = slice(OWN, OWN + size_y)
                    p_now[h, c, slot(face, depth), own, :] = near_now[h, c, place]
                    p_before[h, c, slot(face, depth), own, :] = near_before[h, c, place]
                fill_rows(p_now, p_before, c, slot(face, depth), y_low, y_high, x, size_y)
            for depth in (-1, -2):
                for h in range(halves):
                    zero = jnp.zeros((rows + 8, LANES), jnp.float32)
                    p_now[h, c, slot(face, depth)] = zero
                    p_before[h, c, slot(face, depth)] = zero
        return carry

    lax.fori_loop(0, comps, prepare, 0)

    def give(buf, c, step, offset):
        more = STEPS - 1 - step
        for face in range(2):
            place = slot(face, 0)
            for h in range(halves):
                outs[face][c, h, step * size_y : (step + 1) * size_y, :] = buf[
                    h, c, place, OWN : OWN + size_y, :
                ]
                if more:
                    base = STEPS * size_y + offset
                    outs[face][c, h, base : base + more, :] = buf[h, c, place, OWN - more : OWN, :]
                    outs[face][c, h, base + more : base + 2 * more, :] = buf[
                        h, c, place, OWN + size_y : OWN + size_y + more, :
                    ]

    def evolve(c, carry):
        cur, old = p_now, p_before
        give(cur, c, 0, 0)
        offset = 2 * (STEPS - 1)
        for step, depths in ((1, (-1, 0, 1, 2)), (2, (-1, 0, 1)), (3, (0,))):
            for face in range(2):
                start = OWN - STEPS
                span = range(depths[0] - 1, depths[-1] + 2)
                mids = {d: load(cur, c, slot(face, d), start, rows) for d in span}
                for d in depths:
                    advance(cur, old, c, slot(face, d), mids[d], (mids[d - 1], mids[d + 1]), edges)
            cur, old = old, cur
            give(cur, c, step, offset)
            offset += 2 * (STEPS - 1 - step)
        for face in range(2):
            for h in range(halves):
                base = STEPS * size_y + offset
                outs[face][c, h, base : base + 4, :] = jnp.zeros((4, LANES), jnp.float32)
        return carry

    lax.fori_loop(0, comps, evolve, 0)


def identity(n, dtype):
    row = lax.broadcasted_iota(jnp.int32, (n, n), 0)
    col = lax.broadcasted_iota(jnp.int32, (n, n), 1)
    return (row == col).astype(jnp.float32).astype(dtype)


def turn_tile(read, eye):
    parts = []
    for h in range(eye.shape[0] // LANES):
        cells = read(h)
        parts.append(cells.reshape(-1, LANES).astype(jnp.bfloat16))
    cells = jnp.concatenate(parts, axis=1)
    return lax.dot_general(
        eye, cells, (((1,), (1,)), ((), ())), preferred_element_type=jnp.float32
    )


def fill_spread(spread, comps):
    rows, cols = spread.shape
    per = cols // comps
    part = rows // 2 // comps
    for c in range(comps):
        row = lax.broadcasted_iota(jnp.int32, (rows, per), 0)
        col = lax.broadcasted_iota(jnp.int32, (rows, per), 1) // TILE
        goal = col // part * (rows // 2) + c * part + col % part
        hot = row == goal
        spread[:, c * per : (c + 1) * per] = hot.astype(jnp.float32).astype(jnp.bfloat16)


def spread_tiles(cells_of, spread, lhs, first, comps, group):
    cells = jnp.concatenate([cells_of(first + b) for b in range(group)], axis=0)
    cells = cells.astype(jnp.bfloat16)
    per = lhs.shape[2]
    row = lax.broadcasted_iota(jnp.int32, (TILE, per), 0)
    col = lax.broadcasted_iota(jnp.int32, (TILE, per), 1) % TILE
    keep = row == col
    for pair in range(comps // 2):
        wide = [
            jnp.dot(
                cells, spread[:, c * per : (c + 1) * per], preferred_element_type=jnp.float32
            )
            for c in (2 * pair, 2 * pair + 1)
        ]
        for b in range(group):
            both = [jnp.where(keep, w[b * TILE : (b + 1) * TILE], 0.0) for w in wide]
            lhs[first + b, pair * 2 * TILE : (pair + 1) * 2 * TILE, :] = jnp.concatenate(
                both, axis=0
            ).astype(jnp.bfloat16)


SPREAD = 32
GROUP = 8


def panel_rows(lhs, weights, comps):
    panels = []
    height = comps * TILE
    for b in range(0, len(lhs), 2):
        left = jnp.concatenate([lhs[b], lhs[b + 1]], axis=0)
        right = jnp.concatenate([weights[b], weights[b + 1]], axis=1)
        made = jnp.dot(left, right, preferred_element_type=jnp.float32)
        half = made.shape[1] // 2
        for n, m in ((0, made[:height, :half]), (1, made[height:, half:])):
            panels.append(
                [
                    jnp.sum(m[c * TILE : (c + 1) * TILE], axis=0, keepdims=True)
                    for c in range(comps)
                ]
            )
    return panels


def place_kernel(
    block_patch, ownership, now, before, out, place, near_now, near_before, count, sems,
    *, slots, stride,
):
    comps, size_x, _, size_z = now.shape
    copies = []
    for a, (src, dst) in enumerate(((now, near_now), (before, near_before))):
        for face in range(2):
            x0 = 0 if face == 0 else size_x - STEPS
            for h in range(size_z // LANES):
                copies.append(
                    pltpu.make_async_copy(
                        src.at[:, x0 : x0 + STEPS, :, h * LANES : (h + 1) * LANES],
                        dst.at[h, :, face * STEPS : (face + 1) * STEPS],
                        sems.at[a, face, h],
                    )
                )
    for copy in copies:
        copy.start()
    blocks = block_patch.shape[0]
    devices = lax.axis_size("bx") * lax.axis_size("by")
    owned = ownership.shape[0] // devices
    out[...] = jnp.full(out.shape, -1.0, jnp.float32)

    def clear(d, carry):
        count[d] = 0
        return carry

    lax.fori_loop(0, devices, clear, 0, unroll=8)

    def one(b, carry):
        target = ownership[block_patch[b]]
        owner = target // owned
        rank = count[owner]
        count[owner] = rank + 1
        row = owner * stride + rank
        place[b] = row
        local = (target - owner * owned).astype(jnp.float32)
        out[pl.ds(row + comps * slots, 1), :] = jnp.full((1, LANES), local, jnp.float32)
        return carry

    lax.fori_loop(0, blocks, one, 0, unroll=8)
    for copy in copies:
        copy.wait()


def own_kernel(now, before, y_low, y_high, far, near, p_now, p_before, sems):
    comps, size_x, size_y, size_z = now.shape
    halves = size_z // LANES
    rows = size_y + 2 * STEPS
    tiles_y = size_y // TILE
    tiles_z = size_z // TILE
    columns = size_x // TILE * tiles_y
    copies = []
    for a, (src, dst) in enumerate(((now, p_now), (before, p_before))):
        for h in range(halves):
            copies.append(
                pltpu.make_async_copy(
                    src.at[:, :, :, h * LANES : (h + 1) * LANES],
                    dst.at[h, :, 2 : 2 + size_x, OWN : OWN + size_y, :],
                    sems.at[a, h],
                )
            )
    for copy in copies:
        copy.start()
    edges = edge_rows()
    keep_low = lax.axis_index("bx") > 0
    keep_high = lax.axis_index("bx") < lax.axis_size("bx") - 1

    def prepare(c, carry):
        def one(x, carry):
            fill_rows(p_now, p_before, c, x + 2, y_low, y_high, x, size_y)
            return carry

        lax.fori_loop(0, size_x, one, 0)
        for place in (0, 1, size_x + 2, size_x + 3):
            for h in range(halves):
                zero = jnp.zeros((rows + 8, LANES), jnp.float32)
                p_now[h, c, place] = zero
                p_before[h, c, place] = zero
        return carry

    lax.fori_loop(0, comps, prepare, 0)
    eye = identity(size_z, jnp.bfloat16)
    for copy in copies:
        copy.wait()
    cur, old = p_now, p_before
    for step in range(STEPS):
        out_planes = (1, 2, 1, 0)[step]

        def evolve(c, carry, cur=cur, old=old, out_planes=out_planes, step=step):
            last = step == STEPS - 1
            bounds = None if last else edges
            start, count = (OWN, size_y) if last else (OWN - STEPS, rows)
            first, end = -out_planes, size_x + out_planes
            mids = {}

            def plane(x):
                if x not in mids and -2 <= x < size_x + 2:
                    mids[x] = load(cur, c, x + 2, start, count)
                return mids.get(x)

            for x in range(first, end):
                beside = [p for p in (plane(x - 1), plane(x + 1)) if p is not None]
                keep = keep_low if x < 0 else keep_high if x >= size_x else None
                advance(cur, old, c, x + 2, plane(x), beside, bounds, keep)
                mids.pop(x - 1, None)
            return carry

        lax.fori_loop(0, comps, evolve, 0)

        for column in range(columns):
            face = column // tiles_y
            x0 = 2 + (STEPS if face == 0 else size_x - 2 * STEPS)
            y0 = OWN + column % tiles_y * TILE
            turned = turn_tile(lambda h: old[h, :, x0 : x0 + STEPS, y0 : y0 + TILE, :], eye)
            first = (step * columns + column) * tiles_z
            far[pl.ds(first, tiles_z)] = turned.reshape(tiles_z, TILE, comps * STEPS * TILE)
        for face in range(2):
            x0 = 2 + (0 if face == 0 else size_x - STEPS)
            for h in range(halves):
                near[step, h, :, face * STEPS : (face + 1) * STEPS] = old[
                    h, :, x0 : x0 + STEPS, OWN : OWN + size_y, :
                ]
        cur, old = old, cur


def share_kernel(
    tile_index, step_offset, place, base, from_low, from_high, far, near, weight, out,
    bound, d_now, d_before, table, held, spread, lhs, wsems, *, slots,
):
    _, halves, comps, _, size_y, _ = near.shape
    size_z = halves * LANES
    rows = size_y + 2 * STEPS
    blocks = weight.shape[0]
    tiles_y = size_y // TILE
    tiles_z = size_z // TILE
    columns = 2 * tiles_y

    def weights(g):
        part = pl.ds(g * GROUP, GROUP)
        return pltpu.make_async_copy(weight.at[part], held.at[part], wsems.at[g])

    for g in range(blocks // GROUP):
        weights(g).start()
    out[...] = base[...]
    edges = edge_rows()
    froms = (from_low, from_high)

    def prepare(c, carry):
        for face in range(2):
            offset = STEPS * size_y
            for step in range(STEPS):
                place = face * STEPS + step
                more = STEPS - 1 - step
                for h in range(halves):
                    src = froms[face]
                    bound[h, c, place, OWN : OWN + size_y, :] = src[
                        c, h, step * size_y : (step + 1) * size_y, :
                    ]
                    if more:
                        bound[h, c, place, OWN - more : OWN, :] = src[
                            c, h, offset : offset + more, :
                        ]
                        bound[h, c, place, OWN + size_y : OWN + size_y + more, :] = src[
                            c, h, offset + more : offset + 2 * more, :
                        ]
                offset += 2 * more
            for place in range(face * STEPS, (face + 1) * STEPS):
                for h in range(halves):
                    zero = jnp.zeros((rows + 8, LANES), jnp.float32)
                    d_now[h, c, place] = zero
                    d_before[h, c, place] = zero
        return carry

    lax.fori_loop(0, comps, prepare, 0)
    fill_spread(spread, comps)
    eye = identity(size_z, jnp.bfloat16)

    def slot(face, depth):
        return depth if face == 0 else 2 * STEPS - 1 - depth

    cur, old = d_now, d_before
    for step in range(STEPS):

        def evolve(c, carry, cur=cur, old=old, step=step):
            last = step == STEPS - 1
            bounds = None if last else edges
            start, count = (OWN, size_y) if last else (OWN - STEPS, rows)
            for face in range(2):
                mids = {
                    d: load(cur, c, slot(face, d), start, count)
                    for d in range(min(step + 2, STEPS))
                }
                mids[-1] = load(bound, c, face * STEPS + step, start, count)
                for d in range(step + 1):
                    beside = [mids[x] for x in (d - 1, d + 1) if x in mids]
                    advance(cur, old, c, slot(face, d), mids[d], beside, bounds)
            return carry

        for c in range(comps):
            evolve(c, 0)

        for column in range(columns):
            x0 = column // tiles_y * STEPS
            y0 = column % tiles_y * TILE

            def read(h):
                kept = near[step, h, :, x0 : x0 + STEPS, y0 : y0 + TILE, :]
                return kept + old[h, :, x0 : x0 + STEPS, OWN + y0 : OWN + y0 + TILE, :]

            turned = turn_tile(read, eye)
            first = (step * columns + column) * tiles_z
            table[pl.ds(first, tiles_z)] = turned.reshape(tiles_z, TILE, comps * STEPS * TILE)
        cur, old = old, cur

    def panels(g, carry):
        weights(g).wait()
        made = panel_rows(
            [lhs[g * GROUP + b] for b in range(GROUP)],
            [held[g * GROUP + b] for b in range(GROUP)],
            comps,
        )
        for b in range(GROUP):
            row = place[g * GROUP + b]
            for c in range(comps):
                out[pl.ds(row + c * slots, 1), :] = made[b][c]
        return carry

    def cells_of(block):
        tile = tile_index[block]
        at = step_offset[block] * (columns * tiles_z) + tile
        low = tile < tiles_y * tiles_z
        a, b = table[at], far[at]
        return jnp.concatenate([jnp.where(low, a, b), jnp.where(low, b, a)], axis=1)

    def widen(g, carry):
        spread_tiles(cells_of, spread, lhs, g * SPREAD, comps, SPREAD)
        return carry

    lax.fori_loop(0, blocks // SPREAD, widen, 0)
    lax.fori_loop(0, blocks // GROUP, panels, 0)


PAIRS = 16


def near_kernel(pairs, got, precorrection, out, field, total, held, sems, *, comps, slots, stride):
    count = precorrection.shape[0]
    senders = got.shape[0] // stride
    owned = out.shape[0] // comps

    def blocks(g):
        part = pl.ds(g * PAIRS, PAIRS)
        return pltpu.make_async_copy(precorrection.at[part], held.at[part], sems.at[g])

    for g in range(count // PAIRS):
        blocks(g).start()
    field[...] = jnp.zeros(field.shape, jnp.float32)
    whole = got[...].reshape(senders, stride, LANES)
    ids = whole[:, comps * slots : (comps + 1) * slots, :].reshape(senders * slots, LANES)
    ids = ids.T[:owned]
    hot = ids == lax.broadcasted_iota(jnp.int32, ids.shape, 0).astype(jnp.float32)
    hot = hot.astype(jnp.float32).astype(jnp.bfloat16)
    for c in range(comps):
        rest = whole[:, c * slots : (c + 1) * slots, :].reshape(senders * slots, LANES)
        summed = None
        for _ in range(3):
            piece = rest.astype(jnp.bfloat16)
            rest = rest - piece.astype(jnp.float32)
            part = jnp.dot(hot, piece, preferred_element_type=jnp.float32)
            summed = part if summed is None else summed + part
        field[pl.ds(c, owned, stride=TILE), :] = summed
    total[...] = field[...]
    empty = jnp.zeros((TILE, LANES), jnp.float32)

    def group(g, carry):
        blocks(g).wait()
        made = []
        for b in range(0, PAIRS, 4):
            k = g * PAIRS + b
            rows = []
            for n in range(4):
                source = field[pl.ds(pl.multiple_of(pairs[2 * (k + n) + 1] * TILE, TILE), TILE), :]
                both = [source, empty] if n % 2 == 0 else [empty, source]
                rows.append(jnp.concatenate(both, axis=1))
            left = jnp.concatenate(rows, axis=0).astype(jnp.bfloat16)
            right = jnp.concatenate(
                [
                    jnp.concatenate([held[k], held[k + 2]], axis=1),
                    jnp.concatenate([held[k + 1], held[k + 3]], axis=1),
                ],
                axis=0,
            )
            four = jnp.dot(left, right, preferred_element_type=jnp.float32)
            for n in range(4):
                lane = n // 2 * LANES
                made.append(four[n * TILE : (n + 1) * TILE, lane : lane + LANES])
        for b in range(PAIRS):
            at = pl.ds(pl.multiple_of(pairs[2 * (g * PAIRS + b)] * TILE, TILE), TILE)
            total[at, :] += made[b]
        return carry

    lax.fori_loop(0, count // PAIRS, group, 0)
    for c in range(comps):
        out[pl.ds(c, owned, stride=comps), :] = total[pl.ds(c, owned, stride=TILE), :]


SMEM = pl.BlockSpec(memory_space=pltpu.SMEM)
VMEM = pl.BlockSpec(memory_space=pltpu.VMEM)
HBM = pl.BlockSpec(memory_space=pltpu.HBM)


def in_hbm(a):
    return pltpu.with_memory_space_constraint(a, pltpu.HBM)


def kernel_params(mib):
    return pltpu.CompilerParams(vmem_limit_bytes=mib * MEGA)


def per_device(
    field_now,
    field_before,
    interp_weight,
    tile_index,
    step_offset,
    block_patch,
    ownership,
    near_pairs,
    precorrection,
):
    comps, size_x, size_y, size_z = field_now.shape
    count_x = lax.axis_size("bx")
    count_y = lax.axis_size("by")
    devices = count_x * count_y
    blocks, cells, points = interp_weight.shape
    capacity = max(2, (2 * blocks + devices - 1) // devices)
    owned = ownership.shape[0] // devices
    halves = size_z // LANES
    rows = size_y + 2 * OWN
    f32, bf16 = jnp.float32, jnp.bfloat16

    def swap(up, down, axis, count):
        forward = [(i, i + 1) for i in range(count - 1)]
        backward = [(b, a) for a, b in forward]
        return lax.ppermute(up, axis, forward), lax.ppermute(down, axis, backward)

    slots = ceil8(capacity)
    stride = (comps + 1) * slots
    sent_shape = jax.ShapeDtypeStruct((devices * stride, points), f32)

    last, first = slice(size_y - STEPS, size_y), slice(0, STEPS)
    up = jnp.concatenate([field_now[:, :, last], field_before[:, :, last]], axis=2)
    down = jnp.concatenate([field_now[:, :, first], field_before[:, :, first]], axis=2)
    y_low, y_high = swap(up, down, "by", count_y)

    near_shape = jax.ShapeDtypeStruct((halves, comps, 2 * STEPS, size_y, LANES), f32)
    base, place, near_now, near_before = pl.pallas_call(
        functools.partial(place_kernel, slots=slots, stride=stride),
        out_shape=(
            sent_shape, jax.ShapeDtypeStruct((blocks,), jnp.int32), near_shape, near_shape
        ),
        in_specs=[SMEM, SMEM, HBM, HBM],
        out_specs=(VMEM, SMEM, VMEM, VMEM),
        scratch_shapes=[
            pltpu.SMEM((devices,), jnp.int32), pltpu.SemaphoreType.DMA((2, 2, halves))
        ],
    )(block_patch, ownership, in_hbm(field_now), in_hbm(field_before))

    face_rows = STEPS * size_y + ceil8(STEPS * (STEPS - 1) + 4)
    face = jax.ShapeDtypeStruct((comps, halves, face_rows, LANES), f32)
    plane = pltpu.VMEM((halves, comps, 12, rows, LANES), f32)
    give_low, give_high = pl.pallas_call(
        faces_kernel,
        out_shape=(face, face),
        in_specs=[VMEM, VMEM, VMEM, VMEM],
        out_specs=(VMEM, VMEM),
        scratch_shapes=[plane, plane],
        compiler_params=kernel_params(24),
    )(near_now, near_before, y_low, y_high)
    from_low, from_high = swap(give_high, give_low, "bx", count_x)

    tiles = size_x // TILE * (size_y // TILE) * (size_z // TILE)
    brick = pltpu.VMEM((halves, comps, size_x + 4, rows, LANES), f32)
    half = comps * STEPS * TILE
    far, near = pl.pallas_call(
        own_kernel,
        out_shape=(
            jax.ShapeDtypeStruct((STEPS * tiles, TILE, half), f32),
            jax.ShapeDtypeStruct((STEPS,) + near_shape.shape, f32),
        ),
        in_specs=[HBM, HBM, VMEM, VMEM],
        out_specs=(VMEM, VMEM),
        scratch_shapes=[brick, brick, pltpu.SemaphoreType.DMA((2, halves))],
        compiler_params=kernel_params(24),
    )(in_hbm(field_now), in_hbm(field_before), y_low, y_high)

    thin = pltpu.VMEM((halves, comps, 2 * STEPS, rows, LANES), f32)
    sent = pl.pallas_call(
        functools.partial(share_kernel, slots=slots),
        out_shape=sent_shape,
        in_specs=[SMEM, SMEM, SMEM, VMEM, VMEM, VMEM, VMEM, VMEM, HBM],
        out_specs=VMEM,
        scratch_shapes=[
            thin,
            thin,
            thin,
            pltpu.VMEM((STEPS * tiles, TILE, half), f32),
            pltpu.VMEM((blocks, cells, points), bf16),
            pltpu.VMEM((2 * half, comps * cells), bf16),
            pltpu.VMEM((blocks, comps * TILE, cells), bf16),
            pltpu.SemaphoreType.DMA((blocks // GROUP,)),
        ],
        compiler_params=kernel_params(40),
    )(
        tile_index, step_offset, place, base, from_low, from_high, far, near,
        in_hbm(interp_weight),
    )
    got = lax.all_to_all(
        sent.reshape(devices, stride, points), ("bx", "by"), 0, 0, tiled=True
    ).reshape(devices * stride, points)

    pairs = near_pairs.shape[0]
    result = pl.pallas_call(
        functools.partial(near_kernel, comps=comps, slots=slots, stride=stride),
        out_shape=jax.ShapeDtypeStruct((owned * comps, points), f32),
        in_specs=[SMEM, VMEM, HBM],
        out_specs=VMEM,
        scratch_shapes=[
            pltpu.VMEM((owned * TILE, points), f32),
            pltpu.VMEM((owned * TILE, points), f32),
            pltpu.VMEM((pairs, points, points), bf16),
            pltpu.SemaphoreType.DMA((pairs // PAIRS,)),
        ],
        compiler_params=kernel_params(32),
    )(near_pairs.reshape(-1), got, in_hbm(precorrection))
    return result.reshape(owned, comps, points)


def solution(mesh):
    placed = (
        P(None, "bx", "by", None),
        P(None, "bx", "by", None),
        P(("bx", "by"), None, None),
        P(("bx", "by")),
        P(("bx", "by")),
        P(("bx", "by")),
        P(),
        P(("bx", "by"), None),
        P(("bx", "by"), None, None),
    )
    return jax.shard_map(
        per_device,
        mesh=mesh,
        in_specs=placed,
        out_specs=P(("bx", "by"), None, None),
        check_vma=False,
    )
```

```python
import functools

import jax
import jax.numpy as jnp
from jax import lax
from jax.experimental import pallas as pl
from jax.experimental.pallas import tpu as pltpu
from jax.sharding import PartitionSpec as P

STEPS = 4
COEF = 0.3
LANES = 128
TILE = 8
OWN = 8
MEGA = 1 << 20


def ceil8(n):
    return (n + 7) // 8 * 8


def edge_rows():
    at_low = lax.axis_index("by") == 0
    at_high = lax.axis_index("by") == lax.axis_size("by") - 1
    row = lax.broadcasted_iota(jnp.int32, (8, LANES), 0)
    keep_low = row >= jnp.where(at_low, STEPS, 0)
    keep_high = row < jnp.where(at_high, 8 - STEPS, 8)
    return keep_low, keep_high


def beside_z(mid):
    halves = len(mid)
    lane = lax.broadcasted_iota(jnp.int32, mid[0].shape, 1)
    first = lane == 0
    last = lane == LANES - 1
    up = [pltpu.roll(m, 1, 1) for m in mid]
    down = [pltpu.roll(m, LANES - 1, 1) for m in mid]
    sums = []
    for h in range(halves):
        below = jnp.where(first, up[h - 1] if h else 0.0, up[h])
        above = jnp.where(last, down[h + 1] if h + 1 < halves else 0.0, down[h])
        sums.append(below + above)
    return sums


def load(ref, c, slot, start, rows):
    return [ref[h, c, slot, start : start + rows, :] for h in range(ref.shape[0])]


def advance(cur, old, c, slot, mid, beside, edges, keep=None):
    rows = mid[0].shape[0]
    start = OWN if edges is None else OWN - STEPS
    across = beside_z(mid)
    for h in range(len(mid)):
        total = across[h] + cur[h, c, slot, start - 1 : start - 1 + rows, :]
        total = total + cur[h, c, slot, start + 1 : start + 1 + rows, :]
        for plane in beside:
            total = total + plane[h]
        before = old[h, c, slot, start : start + rows, :]
        fresh = (2.0 - 6.0 * COEF) * mid[h] - before + COEF * total
        if keep is not None:
            fresh = jnp.where(keep, fresh, 0.0)
        if edges is None:
            old[h, c, slot, start : start + rows, :] = fresh
            continue
        old[h, c, slot, start : start + 8, :] = jnp.where(edges[0], fresh[:8], 0.0)
        old[h, c, slot, start + 8 : start + rows - 8, :] = fresh[8 : rows - 8]
        old[h, c, slot, start + rows - 8 : start + rows, :] = jnp.where(
            edges[1], fresh[rows - 8 :], 0.0
        )


def fill_rows(now, before, c, slot, y_low, y_high, x, size_y):
    for h in range(now.shape[0]):
        z = slice(h * LANES, (h + 1) * LANES)
        top = OWN + size_y
        now[h, c, slot, OWN - STEPS : OWN, :] = y_low[c, x, :STEPS, z]
        before[h, c, slot, OWN - STEPS : OWN, :] = y_low[c, x, STEPS:, z]
        now[h, c, slot, top : top + STEPS, :] = y_high[c, x, :STEPS, z]
        before[h, c, slot, top : top + STEPS, :] = y_high[c, x, STEPS:, z]


def faces_kernel(now, before, y_low, y_high, _, out_low, out_high, p_now, p_before, sems):
    comps, size_x, size_y, size_z = now.shape
    halves = size_z // LANES
    rows = size_y + 2 * STEPS
    near = STEPS
    copies = []
    for a, (src, dst) in enumerate(((now, p_now), (before, p_before))):
        for face in range(2):
            x0 = 0 if face == 0 else size_x - near
            s0 = 2 if face == 0 else 6
            for h in range(halves):
                copies.append(
                    pltpu.make_async_copy(
                        src.at[:, x0 : x0 + near, :, h * LANES : (h + 1) * LANES],
                        dst.at[h, :, s0 : s0 + near, OWN : OWN + size_y, :],
                        sems.at[a, face, h],
                    )
                )
    for copy in copies:
        copy.start()

    def slot(face, depth):
        return depth + 2 if face == 0 else 9 - depth

    edges = edge_rows()
    outs = (out_low, out_high)

    def prepare(c, carry):
        for face in range(2):
            for depth in range(near):
                x = depth if face == 0 else size_x - 1 - depth
                fill_rows(p_now, p_before, c, slot(face, depth), y_low, y_high, x, size_y)
            for depth in (-1, -2):
                for h in range(halves):
                    zero = jnp.zeros((rows + 8, LANES), jnp.float32)
                    p_now[h, c, slot(face, depth)] = zero
                    p_before[h, c, slot(face, depth)] = zero
        return carry

    lax.fori_loop(0, comps, prepare, 0)
    for copy in copies:
        copy.wait()

    def give(buf, c, step, offset):
        more = STEPS - 1 - step
        for face in range(2):
            place = slot(face, 0)
            for h in range(halves):
                outs[face][c, h, step * size_y : (step + 1) * size_y, :] = buf[
                    h, c, place, OWN : OWN + size_y, :
                ]
                if more:
                    base = STEPS * size_y + offset
                    outs[face][c, h, base : base + more, :] = buf[h, c, place, OWN - more : OWN, :]
                    outs[face][c, h, base + more : base + 2 * more, :] = buf[
                        h, c, place, OWN + size_y : OWN + size_y + more, :
                    ]

    def evolve(c, carry):
        cur, old = p_now, p_before
        give(cur, c, 0, 0)
        offset = 2 * (STEPS - 1)
        for step, depths in ((1, (-1, 0, 1, 2)), (2, (-1, 0, 1)), (3, (0,))):
            for face in range(2):
                start = OWN - STEPS
                span = range(depths[0] - 1, depths[-1] + 2)
                mids = {d: load(cur, c, slot(face, d), start, rows) for d in span}
                for d in depths:
                    advance(cur, old, c, slot(face, d), mids[d], (mids[d - 1], mids[d + 1]), edges)
            cur, old = old, cur
            give(cur, c, step, offset)
            offset += 2 * (STEPS - 1 - step)
        for face in range(2):
            for h in range(halves):
                base = STEPS * size_y + offset
                outs[face][c, h, base : base + 4, :] = jnp.zeros((4, LANES), jnp.float32)
        return carry

    lax.fori_loop(0, comps, evolve, 0)


def identity(n, dtype):
    row = lax.broadcasted_iota(jnp.int32, (n, n), 0)
    col = lax.broadcasted_iota(jnp.int32, (n, n), 1)
    return (row == col).astype(jnp.float32).astype(dtype)


def turn_tile(read, eye):
    parts = []
    for h in range(eye.shape[0] // LANES):
        cells = read(h)
        parts.append(cells.reshape(-1, LANES).astype(jnp.bfloat16))
    cells = jnp.concatenate(parts, axis=1)
    return lax.dot_general(
        eye, cells, (((1,), (1,)), ((), ())), preferred_element_type=jnp.float32
    )


def fill_spread(spread, comps):
    rows, cols = spread.shape
    per = cols // comps
    part = rows // 2 // comps
    for c in range(comps):
        row = lax.broadcasted_iota(jnp.int32, (rows, per), 0)
        col = lax.broadcasted_iota(jnp.int32, (rows, per), 1) // TILE
        goal = col // part * (rows // 2) + c * part + col % part
        hot = row == goal
        spread[:, c * per : (c + 1) * per] = hot.astype(jnp.float32).astype(jnp.bfloat16)


def spread_tiles(cells_of, spread, lhs, first, comps, group):
    cells = jnp.concatenate([cells_of(first + b) for b in range(group)], axis=0)
    cells = cells.astype(jnp.bfloat16)
    per = lhs.shape[2]
    row = lax.broadcasted_iota(jnp.int32, (TILE, per), 0)
    col = lax.broadcasted_iota(jnp.int32, (TILE, per), 1) % TILE
    keep = row == col
    for pair in range(comps // 2):
        wide = [
            jnp.dot(
                cells, spread[:, c * per : (c + 1) * per], preferred_element_type=jnp.float32
            )
            for c in (2 * pair, 2 * pair + 1)
        ]
        for b in range(group):
            both = [jnp.where(keep, w[b * TILE : (b + 1) * TILE], 0.0) for w in wide]
            lhs[first + b, pair * 2 * TILE : (pair + 1) * 2 * TILE, :] = jnp.concatenate(
                both, axis=0
            ).astype(jnp.bfloat16)


SPREAD = 32
FETCH = 8
GROUP = 32


def panel_rows(lhs, weights, comps):
    made = [jnp.dot(a, w, preferred_element_type=jnp.float32) for a, w in zip(lhs, weights)]
    return [
        [jnp.sum(m[c * TILE : (c + 1) * TILE], axis=0, keepdims=True) for c in range(comps)]
        for m in made
    ]


def place_kernel(block_patch, ownership, out, place, count, *, comps, slots, stride):
    blocks = block_patch.shape[0]
    devices = lax.axis_size("bx") * lax.axis_size("by")
    owned = ownership.shape[0] // devices
    out[...] = jnp.full(out.shape, -1.0, jnp.float32)

    def clear(d, carry):
        count[d] = 0
        return carry

    lax.fori_loop(0, devices, clear, 0, unroll=8)

    lane = lax.broadcasted_iota(jnp.int32, (1, LANES), 1)

    def one(b, carry):
        target = ownership[block_patch[b]]
        owner = target // owned
        rank = count[owner]
        count[owner] = rank + 1
        row = owner * stride + rank
        place[b] = row
        local = (target - owner * owned).astype(jnp.float32)
        at = pl.ds(owner * stride + comps * slots, 1)
        out[at, :] = jnp.where(lane == rank, local, out[at, :])
        return carry

    lax.fori_loop(0, blocks, one, 0, unroll=8)


def own_kernel(
    now, before, y_low, y_high, weight, far, near, held, p_now, p_before, sems, wsems
):
    comps, size_x, size_y, size_z = now.shape
    halves = size_z // LANES
    rows = size_y + 2 * STEPS
    tiles_y = size_y // TILE
    tiles_z = size_z // TILE
    columns = size_x // TILE * tiles_y
    copies = []
    for a, (src, dst) in enumerate(((now, p_now), (before, p_before))):
        for h in range(halves):
            copies.append(
                pltpu.make_async_copy(
                    src.at[:, :, :, h * LANES : (h + 1) * LANES],
                    dst.at[h, :, 2 : 2 + size_x, OWN : OWN + size_y, :],
                    sems.at[a, h],
                )
            )
    for copy in copies:
        copy.start()
    blocks = weight.shape[0]
    fetches = [
        pltpu.make_async_copy(
            weight.at[g * FETCH : (g + 1) * FETCH], held.at[g * FETCH : (g + 1) * FETCH], wsems.at[g]
        )
        for g in range(blocks // FETCH)
    ]
    for fetch in fetches:
        fetch.start()
    edges = edge_rows()
    keep_low = lax.axis_index("bx") > 0
    keep_high = lax.axis_index("bx") < lax.axis_size("bx") - 1

    def prepare(c, carry):
        def one(x, carry):
            fill_rows(p_now, p_before, c, x + 2, y_low, y_high, x, size_y)
            return carry

        lax.fori_loop(0, size_x, one, 0)
        for place in (0, 1, size_x + 2, size_x + 3):
            for h in range(halves):
                zero = jnp.zeros((rows + 8, LANES), jnp.float32)
                p_now[h, c, place] = zero
                p_before[h, c, place] = zero
        return carry

    lax.fori_loop(0, comps, prepare, 0)
    eye = identity(size_z, jnp.bfloat16)
    for copy in copies:
        copy.wait()
    cur, old = p_now, p_before
    for step in range(STEPS):
        out_planes = (1, 2, 1, 0)[step]

        def evolve(c, carry, cur=cur, old=old, out_planes=out_planes, step=step):
            last = step == STEPS - 1
            bounds = None if last else edges
            start, count = (OWN, size_y) if last else (OWN - STEPS, rows)
            first, end = -out_planes, size_x + out_planes
            mids = {}

            def plane(x):
                if x not in mids and -2 <= x < size_x + 2:
                    mids[x] = load(cur, c, x + 2, start, count)
                return mids.get(x)

            for x in range(first, end):
                beside = [p for p in (plane(x - 1), plane(x + 1)) if p is not None]
                keep = keep_low if x < 0 else keep_high if x >= size_x else None
                advance(cur, old, c, x + 2, plane(x), beside, bounds, keep)
                mids.pop(x - 1, None)
            return carry

        lax.fori_loop(0, comps, evolve, 0)

        for column in range(columns):
            face = column // tiles_y
            x0 = 2 + (STEPS if face == 0 else size_x - 2 * STEPS)
            y0 = OWN + column % tiles_y * TILE
            turned = turn_tile(lambda h: old[h, :, x0 : x0 + STEPS, y0 : y0 + TILE, :], eye)
            first = (step * columns + column) * tiles_z
            far[pl.ds(first, tiles_z)] = turned.reshape(tiles_z, TILE, comps * STEPS * TILE)
        for face in range(2):
            x0 = 2 + (0 if face == 0 else size_x - STEPS)
            for h in range(halves):
                near[step, h, :, face * STEPS : (face + 1) * STEPS] = old[
                    h, :, x0 : x0 + STEPS, OWN : OWN + size_y, :
                ]
        cur, old = old, cur
    for fetch in fetches:
        fetch.wait()


def share_kernel(
    tile_index, step_offset, place, base, from_low, from_high, far, near, held, out,
    bound, d_now, d_before, table, spread, lhs, *, slots,
):
    _, halves, comps, _, size_y, _ = near.shape
    size_z = halves * LANES
    rows = size_y + 2 * STEPS
    blocks = held.shape[0]
    tiles_y = size_y // TILE
    tiles_z = size_z // TILE
    columns = 2 * tiles_y

    out[...] = base[...]
    edges = edge_rows()
    froms = (from_low, from_high)

    def prepare(c, carry):
        for face in range(2):
            offset = STEPS * size_y
            for step in range(STEPS):
                place = face * STEPS + step
                more = STEPS - 1 - step
                for h in range(halves):
                    src = froms[face]
                    bound[h, c, place, OWN : OWN + size_y, :] = src[
                        c, h, step * size_y : (step + 1) * size_y, :
                    ]
                    if more:
                        bound[h, c, place, OWN - more : OWN, :] = src[
                            c, h, offset : offset + more, :
                        ]
                        bound[h, c, place, OWN + size_y : OWN + size_y + more, :] = src[
                            c, h, offset + more : offset + 2 * more, :
                        ]
                offset += 2 * more
            for place in range(face * STEPS, (face + 1) * STEPS):
                for h in range(halves):
                    zero = jnp.zeros((rows + 8, LANES), jnp.float32)
                    d_now[h, c, place] = zero
                    d_before[h, c, place] = zero
        return carry

    lax.fori_loop(0, comps, prepare, 0)
    fill_spread(spread, comps)
    eye = identity(size_z, jnp.bfloat16)

    def slot(face, depth):
        return depth if face == 0 else 2 * STEPS - 1 - depth

    cur, old = d_now, d_before
    for step in range(STEPS):

        def evolve(c, carry, cur=cur, old=old, step=step):
            last = step == STEPS - 1
            bounds = None if last else edges
            start, count = (OWN, size_y) if last else (OWN - STEPS, rows)
            for face in range(2):
                mids = {
                    d: load(cur, c, slot(face, d), start, count)
                    for d in range(min(step + 2, STEPS))
                }
                mids[-1] = load(bound, c, face * STEPS + step, start, count)
                for d in range(step + 1):
                    beside = [mids[x] for x in (d - 1, d + 1) if x in mids]
                    advance(cur, old, c, slot(face, d), mids[d], beside, bounds)
            return carry

        for c in range(comps):
            evolve(c, 0)

        for column in range(columns):
            x0 = column // tiles_y * STEPS
            y0 = column % tiles_y * TILE

            def read(h):
                kept = near[step, h, :, x0 : x0 + STEPS, y0 : y0 + TILE, :]
                return kept + old[h, :, x0 : x0 + STEPS, OWN + y0 : OWN + y0 + TILE, :]

            turned = turn_tile(read, eye)
            first = (step * columns + column) * tiles_z
            table[pl.ds(first, tiles_z)] = turned.reshape(tiles_z, TILE, comps * STEPS * TILE)
        cur, old = old, cur

    def panels(g, carry):
        made = panel_rows(
            [lhs[g * GROUP + b] for b in range(GROUP)],
            [held[g * GROUP + b] for b in range(GROUP)],
            comps,
        )
        for b in range(GROUP):
            row = place[g * GROUP + b]
            for c in range(comps):
                out[pl.ds(row + c * slots, 1), :] = made[b][c]
        return carry

    def cells_of(block):
        tile = tile_index[block]
        at = step_offset[block] * (columns * tiles_z) + tile
        low = tile < tiles_y * tiles_z
        a, b = table[at], far[at]
        return jnp.concatenate([jnp.where(low, a, b), jnp.where(low, b, a)], axis=1)

    def widen(g, carry):
        spread_tiles(cells_of, spread, lhs, g * SPREAD, comps, SPREAD)
        return carry

    lax.fori_loop(0, blocks // SPREAD, widen, 0)
    lax.fori_loop(0, blocks // GROUP, panels, 0)


PAIRS = 32


def near_kernel(pairs, got, precorrection, out, field, total, held, sems, *, comps, slots, stride):
    count = precorrection.shape[0]
    senders = got.shape[0] // stride
    owned = out.shape[0] // comps

    def blocks(g):
        part = pl.ds(g * PAIRS, PAIRS)
        return pltpu.make_async_copy(precorrection.at[part], held.at[part], sems.at[g])

    for g in range(count // PAIRS):
        blocks(g).start()
    field[...] = jnp.zeros(field.shape, jnp.float32)
    def rows_of(first, count):
        return jnp.concatenate(
            [got[n * stride + first : n * stride + first + count, :] for n in range(senders)],
            axis=0,
        )

    wide = senders * slots
    lane = lax.broadcasted_iota(jnp.int32, (LANES, wide), 0)
    goal = lax.broadcasted_iota(jnp.int32, (LANES, wide), 1) % slots
    pick = (lane == goal).astype(jnp.float32).astype(jnp.bfloat16)
    ids = jnp.dot(
        got[pl.ds(comps * slots, senders, stride=stride), :].astype(jnp.bfloat16),
        pick,
        preferred_element_type=jnp.float32,
    )
    sender = lax.broadcasted_iota(jnp.int32, ids.shape, 0)
    goal = lax.broadcasted_iota(jnp.int32, ids.shape, 1) // slots
    ids = jnp.sum(jnp.where(sender == goal, ids, 0.0), axis=0, keepdims=True)
    hot = ids == lax.broadcasted_iota(jnp.int32, (owned, wide), 0).astype(jnp.float32)
    hot = hot.astype(jnp.float32).astype(jnp.bfloat16)
    for c in range(comps):
        rest = rows_of(c * slots, slots)
        summed = None
        for _ in range(3):
            piece = rest.astype(jnp.bfloat16)
            rest = rest - piece.astype(jnp.float32)
            part = jnp.dot(hot, piece, preferred_element_type=jnp.float32)
            summed = part if summed is None else summed + part
        field[pl.ds(c, owned, stride=TILE), :] = summed
    total[...] = field[...]
    empty = jnp.zeros((TILE, LANES), jnp.float32)

    def group(g, carry):
        blocks(g).wait()
        made = []
        for b in range(0, PAIRS, 4):
            k = g * PAIRS + b
            rows = []
            for n in range(4):
                source = field[pl.ds(pl.multiple_of(pairs[2 * (k + n) + 1] * TILE, TILE), TILE), :]
                both = [source, empty] if n % 2 == 0 else [empty, source]
                rows.append(jnp.concatenate(both, axis=1))
            left = jnp.concatenate(rows, axis=0).astype(jnp.bfloat16)
            right = jnp.concatenate(
                [
                    jnp.concatenate([held[k], held[k + 2]], axis=1),
                    jnp.concatenate([held[k + 1], held[k + 3]], axis=1),
                ],
                axis=0,
            )
            four = jnp.dot(left, right, preferred_element_type=jnp.float32)
            for n in range(4):
                lane = n // 2 * LANES
                made.append(four[n * TILE : (n + 1) * TILE, lane : lane + LANES])
        for b in range(PAIRS):
            at = pl.ds(pl.multiple_of(pairs[2 * (g * PAIRS + b)] * TILE, TILE), TILE)
            total[at, :] += made[b]
        return carry

    lax.fori_loop(0, count // PAIRS, group, 0)
    for c in range(comps):
        out[pl.ds(c, owned, stride=comps), :] = total[pl.ds(c, owned, stride=TILE), :]


SMEM = pl.BlockSpec(memory_space=pltpu.SMEM)
VMEM = pl.BlockSpec(memory_space=pltpu.VMEM)
HBM = pl.BlockSpec(memory_space=pltpu.HBM)


def in_hbm(a):
    return pltpu.with_memory_space_constraint(a, pltpu.HBM)


def kernel_params(mib):
    return pltpu.CompilerParams(vmem_limit_bytes=mib * MEGA)


def per_device(
    field_now,
    field_before,
    interp_weight,
    tile_index,
    step_offset,
    block_patch,
    ownership,
    near_pairs,
    precorrection,
):
    comps, size_x, size_y, size_z = field_now.shape
    count_x = lax.axis_size("bx")
    count_y = lax.axis_size("by")
    devices = count_x * count_y
    blocks, cells, points = interp_weight.shape
    capacity = max(2, (2 * blocks + devices - 1) // devices)
    owned = ownership.shape[0] // devices
    halves = size_z // LANES
    rows = size_y + 2 * OWN
    f32, bf16 = jnp.float32, jnp.bfloat16

    def swap(up, down, axis, count):
        forward = [(i, i + 1) for i in range(count - 1)]
        backward = [(b, a) for a, b in forward]
        return lax.ppermute(up, axis, forward), lax.ppermute(down, axis, backward)

    slots = ceil8(capacity)
    stride = comps * slots + 1
    sent_shape = jax.ShapeDtypeStruct((devices * stride, points), f32)

    last, first = slice(size_y - STEPS, size_y), slice(0, STEPS)
    up = jnp.concatenate([field_now[:, :, last], field_before[:, :, last]], axis=2)
    down = jnp.concatenate([field_now[:, :, first], field_before[:, :, first]], axis=2)
    y_low, y_high = swap(up, down, "by", count_y)

    near_shape = jax.ShapeDtypeStruct((halves, comps, 2 * STEPS, size_y, LANES), f32)
    base, place = pl.pallas_call(
        functools.partial(place_kernel, comps=comps, slots=slots, stride=stride),
        out_shape=(sent_shape, jax.ShapeDtypeStruct((blocks,), jnp.int32)),
        in_specs=[SMEM, SMEM],
        out_specs=(VMEM, SMEM),
        scratch_shapes=[pltpu.SMEM((devices,), jnp.int32)],
    )(block_patch, ownership)

    face_rows = STEPS * size_y + ceil8(STEPS * (STEPS - 1) + 4)
    face = jax.ShapeDtypeStruct((comps, halves, face_rows, LANES), f32)
    plane = pltpu.VMEM((halves, comps, 12, rows, LANES), f32)
    give_low, give_high = pl.pallas_call(
        faces_kernel,
        out_shape=(face, face),
        in_specs=[HBM, HBM, VMEM, VMEM, HBM],
        out_specs=(VMEM, VMEM),
        scratch_shapes=[plane, plane, pltpu.SemaphoreType.DMA((2, 2, halves))],
        compiler_params=kernel_params(24),
    )(in_hbm(field_now), in_hbm(field_before), y_low, y_high, in_hbm(base))
    from_low, from_high = swap(give_high, give_low, "bx", count_x)

    tiles = size_x // TILE * (size_y // TILE) * (size_z // TILE)
    brick = pltpu.VMEM((halves, comps, size_x + 4, rows, LANES), f32)
    half = comps * STEPS * TILE
    far, near, held = pl.pallas_call(
        own_kernel,
        out_shape=(
            jax.ShapeDtypeStruct((STEPS * tiles, TILE, half), f32),
            jax.ShapeDtypeStruct((STEPS, halves, comps, 2 * STEPS, size_y, LANES), f32),
            jax.ShapeDtypeStruct(interp_weight.shape, bf16),
        ),
        in_specs=[HBM, HBM, VMEM, VMEM, HBM],
        out_specs=(VMEM, VMEM, VMEM),
        scratch_shapes=[
            brick,
            brick,
            pltpu.SemaphoreType.DMA((2, halves)),
            pltpu.SemaphoreType.DMA((blocks // FETCH,)),
        ],
        compiler_params=kernel_params(18),
    )(in_hbm(field_now), in_hbm(field_before), y_low, y_high, in_hbm(interp_weight))

    thin = pltpu.VMEM((halves, comps, 2 * STEPS, rows, LANES), f32)
    sent = pl.pallas_call(
        functools.partial(share_kernel, slots=slots),
        out_shape=sent_shape,
        in_specs=[SMEM, SMEM, SMEM, VMEM, VMEM, VMEM, VMEM, VMEM, VMEM],
        out_specs=VMEM,
        scratch_shapes=[
            thin,
            thin,
            thin,
            pltpu.VMEM((STEPS * tiles, TILE, half), f32),
            pltpu.VMEM((2 * half, comps * cells), bf16),
            pltpu.VMEM((blocks, comps * TILE, cells), bf16),
        ],
        compiler_params=kernel_params(20),
    )(tile_index, step_offset, place, base, from_low, from_high, far, near, held)
    got = lax.all_to_all(
        sent.reshape(devices, 1, stride * points), ("bx", "by"), 0, 0, tiled=True
    ).reshape(devices * stride, points)

    pairs = near_pairs.shape[0]
    result = pl.pallas_call(
        functools.partial(near_kernel, comps=comps, slots=slots, stride=stride),
        out_shape=jax.ShapeDtypeStruct((owned * comps, points), f32),
        in_specs=[SMEM, VMEM, HBM],
        out_specs=VMEM,
        scratch_shapes=[
            pltpu.VMEM((owned * TILE, points), f32),
            pltpu.VMEM((owned * TILE, points), f32),
            pltpu.VMEM((pairs, points, points), bf16),
            pltpu.SemaphoreType.DMA((pairs // PAIRS,)),
        ],
        compiler_params=kernel_params(32),
    )(near_pairs.reshape(-1), got, in_hbm(precorrection))
    return result.reshape(owned, comps, points)


def solution(mesh):
    placed = (
        P(None, "bx", "by", None),
        P(None, "bx", "by", None),
        P(("bx", "by"), None, None),
        P(("bx", "by")),
        P(("bx", "by")),
        P(("bx", "by")),
        P(),
        P(("bx", "by"), None),
        P(("bx", "by"), None, None),
    )
    return jax.shard_map(
        per_device,
        mesh=mesh,
        in_specs=placed,
        out_specs=P(("bx", "by"), None, None),
        check_vma=False,
    )
```

```python
import functools

import jax
import jax.numpy as jnp
from jax import lax
from jax.experimental import pallas as pl
from jax.experimental.pallas import tpu as pltpu
from jax.sharding import PartitionSpec as P

STEPS = 4
COEF = 0.3
LANES = 128
TILE = 8
OWN = 8
MEGA = 1 << 20


def ceil8(n):
    return (n + 7) // 8 * 8


def edge_rows():
    at_low = lax.axis_index("by") == 0
    at_high = lax.axis_index("by") == lax.axis_size("by") - 1
    row = lax.broadcasted_iota(jnp.int32, (8, LANES), 0)
    keep_low = row >= jnp.where(at_low, STEPS, 0)
    keep_high = row < jnp.where(at_high, 8 - STEPS, 8)
    return keep_low, keep_high


def beside_z(mid):
    halves = len(mid)
    lane = lax.broadcasted_iota(jnp.int32, mid[0].shape, 1)
    first = lane == 0
    last = lane == LANES - 1
    up = [pltpu.roll(m, 1, 1) for m in mid]
    down = [pltpu.roll(m, LANES - 1, 1) for m in mid]
    sums = []
    for h in range(halves):
        below = jnp.where(first, up[h - 1] if h else 0.0, up[h])
        above = jnp.where(last, down[h + 1] if h + 1 < halves else 0.0, down[h])
        sums.append(below + above)
    return sums


def load(ref, c, slot, start, rows):
    return [ref[h, c, slot, start : start + rows, :] for h in range(ref.shape[0])]


def advance(cur, old, c, slot, mid, beside, edges, keep=None):
    rows = mid[0].shape[0]
    start = OWN if edges is None else OWN - STEPS
    across = beside_z(mid)
    for h in range(len(mid)):
        total = across[h] + cur[h, c, slot, start - 1 : start - 1 + rows, :]
        total = total + cur[h, c, slot, start + 1 : start + 1 + rows, :]
        for plane in beside:
            total = total + plane[h]
        before = old[h, c, slot, start : start + rows, :]
        fresh = (2.0 - 6.0 * COEF) * mid[h] - before + COEF * total
        if keep is not None:
            fresh = jnp.where(keep, fresh, 0.0)
        if edges is None:
            old[h, c, slot, start : start + rows, :] = fresh
            continue
        old[h, c, slot, start : start + 8, :] = jnp.where(edges[0], fresh[:8], 0.0)
        old[h, c, slot, start + 8 : start + rows - 8, :] = fresh[8 : rows - 8]
        old[h, c, slot, start + rows - 8 : start + rows, :] = jnp.where(
            edges[1], fresh[rows - 8 :], 0.0
        )


def fill_rows(now, before, c, slot, y_low, y_high, x, size_y):
    for h in range(now.shape[0]):
        z = slice(h * LANES, (h + 1) * LANES)
        top = OWN + size_y
        now[h, c, slot, OWN - STEPS : OWN, :] = y_low[c, x, :STEPS, z]
        before[h, c, slot, OWN - STEPS : OWN, :] = y_low[c, x, STEPS:, z]
        now[h, c, slot, top : top + STEPS, :] = y_high[c, x, :STEPS, z]
        before[h, c, slot, top : top + STEPS, :] = y_high[c, x, STEPS:, z]


def pack_kernel(now, before, face_up, face_down, core_up, core_down, edge, sems):
    comps, size_x, size_y, _ = now.shape
    near = STEPS - 1
    copies = []
    for a, src in enumerate((now, before)):
        for side, row in enumerate((0, size_y - TILE)):
            copies.append(
                pltpu.make_async_copy(
                    src.at[:, :, row : row + TILE, :], edge.at[a, side], sems.at[a, side]
                )
            )
    for copy in copies:
        copy.start()
    for copy in copies:
        copy.wait()

    def one(c, carry):
        for side, face, core in ((0, face_down, core_down), (1, face_up, core_up)):
            rows = slice(side * STEPS, (side + 1) * STEPS)
            for a in range(2):
                out = slice(a * STEPS, (a + 1) * STEPS)
                face[c, :near, out, :] = edge[a, side, c, :near, rows, :]
                face[c, near:, out, :] = edge[a, side, c, size_x - near :, rows, :]
                core[c, :, out, :] = edge[a, side, c, near : size_x - near, rows, :]
        return carry

    lax.fori_loop(0, comps, one, 0)


def faces_kernel(now, before, y_low, y_high, out_low, out_high, p_now, p_before, sems):
    comps, size_x, size_y, size_z = now.shape
    halves = size_z // LANES
    rows = size_y + 2 * STEPS
    near = STEPS
    copies = []
    for a, (src, dst) in enumerate(((now, p_now), (before, p_before))):
        for face in range(2):
            x0 = 0 if face == 0 else size_x - near
            s0 = 2 if face == 0 else 6
            for h in range(halves):
                copies.append(
                    pltpu.make_async_copy(
                        src.at[:, x0 : x0 + near, :, h * LANES : (h + 1) * LANES],
                        dst.at[h, :, s0 : s0 + near, OWN : OWN + size_y, :],
                        sems.at[a, face, h],
                    )
                )
    for copy in copies:
        copy.start()

    def slot(face, depth):
        return depth + 2 if face == 0 else 9 - depth

    edges = edge_rows()
    outs = (out_low, out_high)

    def prepare(c, carry):
        for face in range(2):
            for depth in range(near - 1):
                x = depth if face == 0 else 2 * (near - 1) - 1 - depth
                fill_rows(p_now, p_before, c, slot(face, depth), y_low, y_high, x, size_y)
            for h in range(halves):
                zero = jnp.zeros((STEPS, LANES), jnp.float32)
                for first in (OWN - STEPS, OWN + size_y):
                    p_now[h, c, slot(face, near - 1), first : first + STEPS, :] = zero
                    p_before[h, c, slot(face, near - 1), first : first + STEPS, :] = zero
            for depth in (-1, -2):
                for h in range(halves):
                    zero = jnp.zeros((rows + 8, LANES), jnp.float32)
                    p_now[h, c, slot(face, depth)] = zero
                    p_before[h, c, slot(face, depth)] = zero
        return carry

    lax.fori_loop(0, comps, prepare, 0)
    for copy in copies:
        copy.wait()

    def give(buf, c, step, offset):
        more = STEPS - 1 - step
        for face in range(2):
            place = slot(face, 0)
            for h in range(halves):
                outs[face][c, h, step * size_y : (step + 1) * size_y, :] = buf[
                    h, c, place, OWN : OWN + size_y, :
                ]
                if more:
                    base = STEPS * size_y + offset
                    outs[face][c, h, base : base + more, :] = buf[h, c, place, OWN - more : OWN, :]
                    outs[face][c, h, base + more : base + 2 * more, :] = buf[
                        h, c, place, OWN + size_y : OWN + size_y + more, :
                    ]

    def evolve(c, carry):
        cur, old = p_now, p_before
        give(cur, c, 0, 0)
        offset = 2 * (STEPS - 1)
        for step, depths in ((1, (-1, 0, 1, 2)), (2, (-1, 0, 1)), (3, (0,))):
            for face in range(2):
                start = OWN - STEPS
                span = range(depths[0] - 1, depths[-1] + 2)
                mids = {d: load(cur, c, slot(face, d), start, rows) for d in span}
                for d in depths:
                    advance(cur, old, c, slot(face, d), mids[d], (mids[d - 1], mids[d + 1]), edges)
            cur, old = old, cur
            give(cur, c, step, offset)
            offset += 2 * (STEPS - 1 - step)
        for face in range(2):
            for h in range(halves):
                base = STEPS * size_y + offset
                outs[face][c, h, base : base + 4, :] = jnp.zeros((4, LANES), jnp.float32)
        return carry

    lax.fori_loop(0, comps, evolve, 0)


def identity(n, dtype):
    row = lax.broadcasted_iota(jnp.int32, (n, n), 0)
    col = lax.broadcasted_iota(jnp.int32, (n, n), 1)
    return (row == col).astype(jnp.float32).astype(dtype)


def turn_tile(read, eye):
    parts = []
    for h in range(eye.shape[0] // LANES):
        cells = read(h)
        parts.append(cells.reshape(-1, LANES).astype(jnp.bfloat16))
    cells = jnp.concatenate(parts, axis=1)
    return lax.dot_general(
        eye, cells, (((1,), (1,)), ((), ())), preferred_element_type=jnp.float32
    )


def fill_spread(spread, comps):
    rows, cols = spread.shape
    per = cols // comps
    part = rows // 2 // comps
    for c in range(comps):
        row = lax.broadcasted_iota(jnp.int32, (rows, per), 0)
        col = lax.broadcasted_iota(jnp.int32, (rows, per), 1) // TILE
        goal = col // part * (rows // 2) + c * part + col % part
        hot = row == goal
        spread[:, c * per : (c + 1) * per] = hot.astype(jnp.float32).astype(jnp.bfloat16)


def spread_tiles(cells_of, spread, lhs, first, comps, group):
    cells = jnp.concatenate([cells_of(first + b) for b in range(group)], axis=0)
    cells = cells.astype(jnp.bfloat16)
    per = lhs.shape[2]
    row = lax.broadcasted_iota(jnp.int32, (TILE, per), 0)
    col = lax.broadcasted_iota(jnp.int32, (TILE, per), 1) % TILE
    keep = row == col
    for pair in range(comps // 2):
        wide = [
            jnp.dot(
                cells, spread[:, c * per : (c + 1) * per], preferred_element_type=jnp.float32
            )
            for c in (2 * pair, 2 * pair + 1)
        ]
        for b in range(group):
            both = [jnp.where(keep, w[b * TILE : (b + 1) * TILE], 0.0) for w in wide]
            lhs[first + b, pair * 2 * TILE : (pair + 1) * 2 * TILE, :] = jnp.concatenate(
                both, axis=0
            ).astype(jnp.bfloat16)


SPREAD = 32
FETCH = 8
GROUP = 32


def panel_rows(lhs, weights, comps):
    made = [jnp.dot(a, w, preferred_element_type=jnp.float32) for a, w in zip(lhs, weights)]
    return [
        [jnp.sum(m[c * TILE : (c + 1) * TILE], axis=0, keepdims=True) for c in range(comps)]
        for m in made
    ]


def place_kernel(block_patch, ownership, _, out, place, count, *, comps, slots, stride):
    blocks = block_patch.shape[0]
    devices = lax.axis_size("bx") * lax.axis_size("by")
    owned = ownership.shape[0] // devices
    out[...] = jnp.full(out.shape, -1.0, jnp.float32)

    def clear(d, carry):
        count[d] = 0
        return carry

    lax.fori_loop(0, devices, clear, 0, unroll=8)

    lane = lax.broadcasted_iota(jnp.int32, (1, LANES), 1)

    def one(b, carry):
        target = ownership[block_patch[b]]
        owner = target // owned
        rank = count[owner]
        count[owner] = rank + 1
        row = owner * stride + rank
        place[b] = row
        local = (target - owner * owned).astype(jnp.float32)
        at = pl.ds(owner * stride + comps * slots, 1)
        out[at, :] = jnp.where(lane == rank, local, out[at, :])
        return carry

    lax.fori_loop(0, blocks, one, 0, unroll=8)


def own_kernel(
    now, before, face_low, face_high, core_low, core_high, weight, far, near, held,
    p_now, p_before, sems, wsems,
):
    comps, size_x, size_y, size_z = now.shape
    halves = size_z // LANES
    rows = size_y + 2 * STEPS
    tiles_y = size_y // TILE
    tiles_z = size_z // TILE
    columns = size_x // TILE * tiles_y
    copies = []
    for a, (src, dst) in enumerate(((now, p_now), (before, p_before))):
        for h in range(halves):
            copies.append(
                pltpu.make_async_copy(
                    src.at[:, :, :, h * LANES : (h + 1) * LANES],
                    dst.at[h, :, 2 : 2 + size_x, OWN : OWN + size_y, :],
                    sems.at[a, h],
                )
            )
    for copy in copies:
        copy.start()
    blocks = weight.shape[0]
    fetches = [
        pltpu.make_async_copy(
            weight.at[g * FETCH : (g + 1) * FETCH], held.at[g * FETCH : (g + 1) * FETCH], wsems.at[g]
        )
        for g in range(blocks // FETCH)
    ]
    for fetch in fetches:
        fetch.start()
    edges = edge_rows()
    keep_low = lax.axis_index("bx") > 0
    keep_high = lax.axis_index("bx") < lax.axis_size("bx") - 1

    edge = STEPS - 1

    def prepare(c, carry):
        def one(x, carry):
            fill_rows(p_now, p_before, c, x + 2 + edge, core_low, core_high, x, size_y)
            return carry

        lax.fori_loop(0, size_x - 2 * edge, one, 0)
        for n in range(2 * edge):
            x = n if n < edge else size_x - 2 * edge + n
            fill_rows(p_now, p_before, c, x + 2, face_low, face_high, n, size_y)
        for place in (0, 1, size_x + 2, size_x + 3):
            for h in range(halves):
                zero = jnp.zeros((rows + 8, LANES), jnp.float32)
                p_now[h, c, place] = zero
                p_before[h, c, place] = zero
        return carry

    lax.fori_loop(0, comps, prepare, 0)
    eye = identity(size_z, jnp.bfloat16)
    for copy in copies:
        copy.wait()
    cur, old = p_now, p_before
    for step in range(STEPS):
        out_planes = (1, 2, 1, 0)[step]

        def evolve(c, carry, cur=cur, old=old, out_planes=out_planes, step=step):
            last = step == STEPS - 1
            bounds = None if last else edges
            start, count = (OWN, size_y) if last else (OWN - STEPS, rows)
            first, end = -out_planes, size_x + out_planes
            mids = {}

            def plane(x):
                if x not in mids and -2 <= x < size_x + 2:
                    mids[x] = load(cur, c, x + 2, start, count)
                return mids.get(x)

            for x in range(first, end):
                beside = [p for p in (plane(x - 1), plane(x + 1)) if p is not None]
                keep = keep_low if x < 0 else keep_high if x >= size_x else None
                advance(cur, old, c, x + 2, plane(x), beside, bounds, keep)
                mids.pop(x - 1, None)
            return carry

        lax.fori_loop(0, comps, evolve, 0)

        for column in range(columns):
            face = column // tiles_y
            x0 = 2 + (STEPS if face == 0 else size_x - 2 * STEPS)
            y0 = OWN + column % tiles_y * TILE
            turned = turn_tile(lambda h: old[h, :, x0 : x0 + STEPS, y0 : y0 + TILE, :], eye)
            first = (step * columns + column) * tiles_z
            far[pl.ds(first, tiles_z)] = turned.reshape(tiles_z, TILE, comps * STEPS * TILE)
        for face in range(2):
            x0 = 2 + (0 if face == 0 else size_x - STEPS)
            for h in range(halves):
                near[step, h, :, face * STEPS : (face + 1) * STEPS] = old[
                    h, :, x0 : x0 + STEPS, OWN : OWN + size_y, :
                ]
        cur, old = old, cur
    for fetch in fetches:
        fetch.wait()


def share_kernel(
    tile_index, step_offset, place, base, from_low, from_high, far, near, held, out,
    bound, d_now, d_before, table, spread, lhs, *, slots,
):
    _, halves, comps, _, size_y, _ = near.shape
    size_z = halves * LANES
    rows = size_y + 2 * STEPS
    blocks = held.shape[0]
    tiles_y = size_y // TILE
    tiles_z = size_z // TILE
    columns = 2 * tiles_y

    out[...] = base[...]
    edges = edge_rows()
    froms = (from_low, from_high)

    def prepare(c, carry):
        for face in range(2):
            offset = STEPS * size_y
            for step in range(STEPS):
                place = face * STEPS + step
                more = STEPS - 1 - step
                for h in range(halves):
                    src = froms[face]
                    bound[h, c, place, OWN : OWN + size_y, :] = src[
                        c, h, step * size_y : (step + 1) * size_y, :
                    ]
                    if more:
                        bound[h, c, place, OWN - more : OWN, :] = src[
                            c, h, offset : offset + more, :
                        ]
                        bound[h, c, place, OWN + size_y : OWN + size_y + more, :] = src[
                            c, h, offset + more : offset + 2 * more, :
                        ]
                offset += 2 * more
            for place in range(face * STEPS, (face + 1) * STEPS):
                for h in range(halves):
                    zero = jnp.zeros((rows + 8, LANES), jnp.float32)
                    d_now[h, c, place] = zero
                    d_before[h, c, place] = zero
        return carry

    lax.fori_loop(0, comps, prepare, 0)
    fill_spread(spread, comps)
    eye = identity(size_z, jnp.bfloat16)

    def slot(face, depth):
        return depth if face == 0 else 2 * STEPS - 1 - depth

    cur, old = d_now, d_before
    for step in range(STEPS):

        def evolve(c, carry, cur=cur, old=old, step=step):
            last = step == STEPS - 1
            bounds = None if last else edges
            start, count = (OWN, size_y) if last else (OWN - STEPS, rows)
            for face in range(2):
                mids = {
                    d: load(cur, c, slot(face, d), start, count)
                    for d in range(min(step + 2, STEPS))
                }
                mids[-1] = load(bound, c, face * STEPS + step, start, count)
                for d in range(step + 1):
                    beside = [mids[x] for x in (d - 1, d + 1) if x in mids]
                    advance(cur, old, c, slot(face, d), mids[d], beside, bounds)
            return carry

        for c in range(comps):
            evolve(c, 0)

        for column in range(columns):
            x0 = column // tiles_y * STEPS
            y0 = column % tiles_y * TILE

            def read(h):
                kept = near[step, h, :, x0 : x0 + STEPS, y0 : y0 + TILE, :]
                return kept + old[h, :, x0 : x0 + STEPS, OWN + y0 : OWN + y0 + TILE, :]

            turned = turn_tile(read, eye)
            first = (step * columns + column) * tiles_z
            table[pl.ds(first, tiles_z)] = turned.reshape(tiles_z, TILE, comps * STEPS * TILE)
        cur, old = old, cur

    def panels(g, carry):
        made = panel_rows(
            [lhs[g * GROUP + b] for b in range(GROUP)],
            [held[g * GROUP + b] for b in range(GROUP)],
            comps,
        )
        for b in range(GROUP):
            row = place[g * GROUP + b]
            for c in range(comps):
                out[pl.ds(row + c * slots, 1), :] = made[b][c]
        return carry

    def cells_of(block):
        tile = tile_index[block]
        at = step_offset[block] * (columns * tiles_z) + tile
        low = tile < tiles_y * tiles_z
        a, b = table[at], far[at]
        return jnp.concatenate([jnp.where(low, a, b), jnp.where(low, b, a)], axis=1)

    def widen(g, carry):
        spread_tiles(cells_of, spread, lhs, g * SPREAD, comps, SPREAD)
        return carry

    lax.fori_loop(0, blocks // SPREAD, widen, 0)
    lax.fori_loop(0, blocks // GROUP, panels, 0)


PAIRS = 32


def near_kernel(pairs, got, precorrection, out, field, total, held, sems, *, comps, slots, stride):
    count = precorrection.shape[0]
    senders = got.shape[0] // stride
    owned = out.shape[0] // comps

    def blocks(g):
        part = pl.ds(g * PAIRS, PAIRS)
        return pltpu.make_async_copy(precorrection.at[part], held.at[part], sems.at[g])

    for g in range(count // PAIRS):
        blocks(g).start()
    field[...] = jnp.zeros(field.shape, jnp.float32)
    def rows_of(first, count):
        return jnp.concatenate(
            [got[n * stride + first : n * stride + first + count, :] for n in range(senders)],
            axis=0,
        )

    wide = senders * slots
    lane = lax.broadcasted_iota(jnp.int32, (LANES, wide), 0)
    goal = lax.broadcasted_iota(jnp.int32, (LANES, wide), 1) % slots
    pick = (lane == goal).astype(jnp.float32).astype(jnp.bfloat16)
    ids = jnp.dot(
        got[pl.ds(comps * slots, senders, stride=stride), :].astype(jnp.bfloat16),
        pick,
        preferred_element_type=jnp.float32,
    )
    sender = lax.broadcasted_iota(jnp.int32, ids.shape, 0)
    goal = lax.broadcasted_iota(jnp.int32, ids.shape, 1) // slots
    ids = jnp.sum(jnp.where(sender == goal, ids, 0.0), axis=0, keepdims=True)
    hot = ids == lax.broadcasted_iota(jnp.int32, (owned, wide), 0).astype(jnp.float32)
    hot = hot.astype(jnp.float32).astype(jnp.bfloat16)
    for c in range(comps):
        rest = rows_of(c * slots, slots)
        summed = None
        for _ in range(3):
            piece = rest.astype(jnp.bfloat16)
            rest = rest - piece.astype(jnp.float32)
            part = jnp.dot(hot, piece, preferred_element_type=jnp.float32)
            summed = part if summed is None else summed + part
        field[pl.ds(c, owned, stride=TILE), :] = summed
    total[...] = field[...]
    empty = jnp.zeros((TILE, LANES), jnp.float32)

    def group(g, carry):
        blocks(g).wait()
        made = []
        for b in range(0, PAIRS, 4):
            k = g * PAIRS + b
            rows = []
            for n in range(4):
                source = field[pl.ds(pl.multiple_of(pairs[2 * (k + n) + 1] * TILE, TILE), TILE), :]
                both = [source, empty] if n % 2 == 0 else [empty, source]
                rows.append(jnp.concatenate(both, axis=1))
            left = jnp.concatenate(rows, axis=0).astype(jnp.bfloat16)
            right = jnp.concatenate(
                [
                    jnp.concatenate([held[k], held[k + 2]], axis=1),
                    jnp.concatenate([held[k + 1], held[k + 3]], axis=1),
                ],
                axis=0,
            )
            four = jnp.dot(left, right, preferred_element_type=jnp.float32)
            for n in range(4):
                lane = n // 2 * LANES
                made.append(four[n * TILE : (n + 1) * TILE, lane : lane + LANES])
        for b in range(PAIRS):
            at = pl.ds(pl.multiple_of(pairs[2 * (g * PAIRS + b)] * TILE, TILE), TILE)
            total[at, :] += made[b]
        return carry

    lax.fori_loop(0, count // PAIRS, group, 0)
    for c in range(comps):
        out[pl.ds(c, owned, stride=comps), :] = total[pl.ds(c, owned, stride=TILE), :]


SMEM = pl.BlockSpec(memory_space=pltpu.SMEM)
VMEM = pl.BlockSpec(memory_space=pltpu.VMEM)
HBM = pl.BlockSpec(memory_space=pltpu.HBM)


def in_hbm(a):
    return pltpu.with_memory_space_constraint(a, pltpu.HBM)


def kernel_params(mib):
    return pltpu.CompilerParams(vmem_limit_bytes=mib * MEGA)


def per_device(
    field_now,
    field_before,
    interp_weight,
    tile_index,
    step_offset,
    block_patch,
    ownership,
    near_pairs,
    precorrection,
):
    comps, size_x, size_y, size_z = field_now.shape
    count_x = lax.axis_size("bx")
    count_y = lax.axis_size("by")
    devices = count_x * count_y
    blocks, cells, points = interp_weight.shape
    capacity = max(2, (2 * blocks + devices - 1) // devices)
    owned = ownership.shape[0] // devices
    halves = size_z // LANES
    rows = size_y + 2 * OWN
    f32, bf16 = jnp.float32, jnp.bfloat16

    def swap(up, down, axis, count):
        forward = [(i, i + 1) for i in range(count - 1)]
        backward = [(b, a) for a, b in forward]
        return lax.ppermute(up, axis, forward), lax.ppermute(down, axis, backward)

    slots = ceil8(capacity)
    stride = comps * slots + 1
    sent_shape = jax.ShapeDtypeStruct((devices * stride, points), f32)

    edge = 2 * (STEPS - 1)
    face_rim = jax.ShapeDtypeStruct((comps, edge, 2 * STEPS, size_z), f32)
    core_rim = jax.ShapeDtypeStruct((comps, size_x - edge, 2 * STEPS, size_z), f32)
    face_up, face_down, core_up, core_down = pl.pallas_call(
        pack_kernel,
        out_shape=(face_rim, face_rim, core_rim, core_rim),
        in_specs=[HBM, HBM],
        out_specs=(VMEM, VMEM, VMEM, VMEM),
        scratch_shapes=[
            pltpu.VMEM((2, 2, comps, size_x, TILE, size_z), f32),
            pltpu.SemaphoreType.DMA((2, 2)),
        ],
        compiler_params=kernel_params(16),
    )(in_hbm(field_now), in_hbm(field_before))
    face_low, face_high = swap(face_up, face_down, "by", count_y)
    core_low, core_high = swap(core_up, core_down, "by", count_y)

    face_rows = STEPS * size_y + ceil8(STEPS * (STEPS - 1) + 4)
    face = jax.ShapeDtypeStruct((comps, halves, face_rows, LANES), f32)
    plane = pltpu.VMEM((halves, comps, 12, rows, LANES), f32)
    give_low, give_high = pl.pallas_call(
        faces_kernel,
        out_shape=(face, face),
        in_specs=[HBM, HBM, VMEM, VMEM],
        out_specs=(VMEM, VMEM),
        scratch_shapes=[plane, plane, pltpu.SemaphoreType.DMA((2, 2, halves))],
        cost_estimate=pl.CostEstimate(flops=5000000000, bytes_accessed=5000000, transcendentals=0),
        compiler_params=kernel_params(24),
    )(in_hbm(field_now), in_hbm(field_before), face_low, face_high)
    base, place = pl.pallas_call(
        functools.partial(place_kernel, comps=comps, slots=slots, stride=stride),
        out_shape=(sent_shape, jax.ShapeDtypeStruct((blocks,), jnp.int32)),
        in_specs=[SMEM, SMEM, HBM],
        out_specs=(VMEM, SMEM),
        scratch_shapes=[pltpu.SMEM((devices,), jnp.int32)],
        cost_estimate=pl.CostEstimate(flops=10000000000, bytes_accessed=10000000, transcendentals=0),
    )(block_patch, ownership, in_hbm(give_low))

    from_low, from_high = swap(give_high, give_low, "bx", count_x)

    tiles = size_x // TILE * (size_y // TILE) * (size_z // TILE)
    brick = pltpu.VMEM((halves, comps, size_x + 4, rows, LANES), f32)
    half = comps * STEPS * TILE
    far, near, held = pl.pallas_call(
        own_kernel,
        out_shape=(
            jax.ShapeDtypeStruct((STEPS * tiles, TILE, half), f32),
            jax.ShapeDtypeStruct((STEPS, halves, comps, 2 * STEPS, size_y, LANES), f32),
            jax.ShapeDtypeStruct(interp_weight.shape, bf16),
        ),
        in_specs=[HBM, HBM, VMEM, VMEM, VMEM, VMEM, HBM],
        out_specs=(VMEM, VMEM, VMEM),
        scratch_shapes=[
            brick,
            brick,
            pltpu.SemaphoreType.DMA((2, halves)),
            pltpu.SemaphoreType.DMA((blocks // FETCH,)),
        ],
        cost_estimate=pl.CostEstimate(flops=20000000000, bytes_accessed=20000000, transcendentals=0),
        compiler_params=kernel_params(18),
    )(
        in_hbm(field_now), in_hbm(field_before),
        face_low, face_high, core_low, core_high, in_hbm(interp_weight),
    )

    thin = pltpu.VMEM((halves, comps, 2 * STEPS, rows, LANES), f32)
    sent = pl.pallas_call(
        functools.partial(share_kernel, slots=slots),
        out_shape=sent_shape,
        in_specs=[SMEM, SMEM, SMEM, VMEM, VMEM, VMEM, VMEM, VMEM, VMEM],
        out_specs=VMEM,
        scratch_shapes=[
            thin,
            thin,
            thin,
            pltpu.VMEM((STEPS * tiles, TILE, half), f32),
            pltpu.VMEM((2 * half, comps * cells), bf16),
            pltpu.VMEM((blocks, comps * TILE, cells), bf16),
        ],
        compiler_params=kernel_params(20),
    )(tile_index, step_offset, place, base, from_low, from_high, far, near, held)
    got = lax.all_to_all(
        sent.reshape(devices, 1, stride * points), ("bx", "by"), 0, 0, tiled=True
    ).reshape(devices * stride, points)

    pairs = near_pairs.shape[0]
    result = pl.pallas_call(
        functools.partial(near_kernel, comps=comps, slots=slots, stride=stride),
        out_shape=jax.ShapeDtypeStruct((owned * comps, points), f32),
        in_specs=[SMEM, VMEM, HBM],
        out_specs=VMEM,
        scratch_shapes=[
            pltpu.VMEM((owned * TILE, points), f32),
            pltpu.VMEM((owned * TILE, points), f32),
            pltpu.VMEM((pairs, points, points), bf16),
            pltpu.SemaphoreType.DMA((pairs // PAIRS,)),
        ],
        compiler_params=kernel_params(32),
    )(near_pairs.reshape(-1), got, in_hbm(precorrection))
    return result.reshape(owned, comps, points)


def solution(mesh):
    placed = (
        P(None, "bx", "by", None),
        P(None, "bx", "by", None),
        P(("bx", "by"), None, None),
        P(("bx", "by")),
        P(("bx", "by")),
        P(("bx", "by")),
        P(),
        P(("bx", "by"), None),
        P(("bx", "by"), None, None),
    )
    return jax.shard_map(
        per_device,
        mesh=mesh,
        in_specs=placed,
        out_specs=P(("bx", "by"), None, None),
        check_vma=False,
    )
```
